32 devices in a mesh: seq: 8 (over y, x, core), dp: 4 (over z).
Axes of the slice: x: 2, y: 2, z: 4, core: 2. Of those that a mesh axis runs over, the one named last changes fastest.
Arguments:
- tokens: bfloat16 [4, 1024, 1024], P('dp', 'seq'), may hold values from -8 to 8
- lengths: int32 [4, 3], P('dp'), may hold values from 1 to 682, 1024 in all within a row
- ln1_gain: bfloat16 [1024], P(('seq', 'dp')), may hold values from 0.099609375 to 1.8984375
- q_weight: bfloat16 [1024, 2048], P(('seq', 'dp')), may hold values from -0.1875 to 0.1875
- k_weight: bfloat16 [1024, 1024], P(('seq', 'dp')), may hold values from -0.1875 to 0.1875
- v_weight: bfloat16 [1024, 1024], P(('seq', 'dp')), may hold values from -0.1875 to 0.1875
- attn_gate_weight: bfloat16 [1024, 16], P(('seq', 'dp')), may hold values from -0.1875 to 0.1875
- q_norm_gain: bfloat16 [128], P(('seq', 'dp')), may hold values from 0.5 to 2
- k_norm_gain: bfloat16 [128], P(('seq', 'dp')), may hold values from 0.5 to 2
- o_weight: bfloat16 [2048, 1024], P(('seq', 'dp')), may hold values from -6 to 6
- ln2_gain: bfloat16 [1024], P(('seq', 'dp')), may hold values from 0.099609375 to 1.8984375
- gate_weight: bfloat16 [1024, 3072], P(('seq', 'dp')), may hold values from -0.1875 to 0.1875
- up_weight: bfloat16 [1024, 3072], P(('seq', 'dp')), may hold values from -0.1875 to 0.1875
- down_weight: bfloat16 [3072, 1024], P(('seq', 'dp')), may hold values from -0.109375 to 0.109375
- cotangent: bfloat16 [4, 1024, 1024], P('dp', 'seq'), may hold values from -8 to 8
Outputs:
- layer_out: bfloat16 [4, 1024, 1024], P('dp', 'seq')
- input_grad: float32 [4, 1024, 1024], P('dp', 'seq')
- ln1_grad: float32 [1024], P(('seq', 'dp'))
- q_grad: float32 [1024, 2048], P(('seq', 'dp'))
- k_grad: float32 [1024, 1024], P(('seq', 'dp'))
- v_grad: float32 [1024, 1024], P(('seq', 'dp'))
- attn_gate_grad: float32 [1024, 16], P(('seq', 'dp'))
- q_norm_grad: float32 [128], P(('seq', 'dp'))
- k_norm_grad: float32 [128], P(('seq', 'dp'))
- o_grad: float32 [2048, 1024], P(('seq', 'dp'))
- ln2_grad: float32 [1024], P(('seq', 'dp'))
- gate_grad: float32 [1024, 3072], P(('seq', 'dp'))
- up_grad: float32 [1024, 3072], P(('seq', 'dp'))
- down_grad: float32 [3072, 1024], P(('seq', 'dp'))
The draws below stay inside these ranges and needn't reach their ends.
Inputs may be any that keep to these rules, and one draw needn't show every extreme that they name: Row i holds the lengths of the 3 sequences packed in order into the tokens of index i of dp; they sum to 1024 and the longest is exactly 682.
All inputs are finite; a program needn't handle non-finite values.
Results may differ from the reference program's by a relative error of at most 0.025.
Values may be sent and summed in bfloat16 or wider, within the bound.
No kernel may reach another device: no remote copies, remote signals or barrier semaphores. Data moves between devices by JAX's collectives and lax.ppermute only.
A program may use at most 320 MiB of HBM per device.

```python
import math
import jax
import jax.numpy as jnp
import numpy as np
from jax import lax

D = 1024
FF = 3072
HEADS = 16
KV_HEADS = 8
HEAD_DIM = 128
SEQS = 3
BLOCK = 256
GROUP_TOK = 1024
MOST = 682
N_DP = 4


def spiked(drawn, own_key, source, target, shards_of, factor):
    owner, partner = [(jnp.arange(drawn.shape[dim]) // (drawn.shape[dim] // shards_of)).reshape([-1 if axis == dim else 1 for axis in range(drawn.ndim)]) for dim in (source, target)]
    chosen = jax.random.permutation(own_key, shards_of)[partner]
    strong = (owner == chosen) | (owner == (partner + shards_of // 2) % shards_of)
    return jnp.where(strong, factor * drawn, drawn)


def levels(key, shape, split, smallest, high):
    def one(axis_at, parts):
        heights = jax.random.uniform(jax.random.fold_in(jax.random.fold_in(key, 6), axis_at), (parts,), jnp.float32, smallest / len(split), high / len(split))
        return jnp.repeat(jnp.exp(heights), shape[axis_at] // parts).reshape((-1,) + (1,) * (len(shape) - axis_at - 1))

    gain = one(*split[0])
    for cut in split[1:]:
        gain = gain * one(*cut)
    return gain


def split_up(number_of, total, bound, lean):
    portions = [(1 << 20) // math.isqrt(rank ** lean) + 1 for rank in range(2, number_of + 1)]
    rest, given = total - bound - (number_of - 1), [1] * (number_of - 1)
    while rest > 0:
        free = [i for i in range(number_of - 1) if given[i] < bound]
        pool, budget = sum([portions[i] for i in free]), rest
        for i in free:
            addition = min(bound - given[i], max(1, budget * portions[i] // pool), rest)
            given[i] = given[i] + addition
            rest = rest - addition
    return np.array([bound] + given)


def uneven_parts(rng, amount, total, reach, lean):
    if amount == 2:
        one = jax.random.randint(rng, (), max(1, total - reach), min(reach, total - 1) + 1)
        return jnp.stack([one, total - one])
    sizes = jnp.asarray(split_up(amount, total, reach, lean), jnp.int32)
    couples = (amount - 1) // 2
    source_of, taker = sizes[1:1 + 2 * couples:2], sizes[2:2 + 2 * couples:2]
    margin = jnp.minimum(source_of - 1, reach - taker)
    moved = jax.random.randint(jax.random.fold_in(rng, 1), (couples,), 0, 1 << 20) % (margin + 1)
    sizes = sizes.at[1:1 + 2 * couples:2].set(source_of - moved).at[2:2 + 2 * couples:2].set(taker + moved)
    return sizes[jax.random.permutation(jax.random.fold_in(rng, 2), amount)]


def bell_draw(key, dims, spread, most, split=(), kind=jnp.bfloat16):
    entries = spread * jax.random.normal(key, dims, jnp.float32)
    if split:
        entries = entries * levels(key, dims, split, -0.22, 0.18)
    return jnp.clip(entries, -most, most).astype(kind)


def heavy_noise(stream_key, shape, spread, most, shards, heavy, held_as=jnp.bfloat16):
    array = spread * jax.random.normal(stream_key, shape, jnp.float32)
    if shards:
        array = array * levels(stream_key, shape, shards, -0.22, 0.18)
    return jnp.clip(spiked(array, jax.random.fold_in(stream_key, 3), *heavy), -most, most).astype(held_as)


def setup_inputs(seed: int = 0) -> dict:
    splits = jax.random.split(jax.random.key(seed), 16)
    tokens = heavy_noise(splits[0], (N_DP, GROUP_TOK, D), 1.0, 8.0, ((0, 4), (1, 8)), (1, 2, 8, 2.0))
    lengths = jax.vmap(lambda own: uneven_parts(own, SEQS, GROUP_TOK, MOST, 1))(jax.random.split(splits[1], N_DP)).reshape((N_DP, SEQS)).astype(jnp.int32)
    ln1_gain = jnp.clip(1.0 + 0.18 * jax.random.normal(splits[2], (D,), jnp.float32), 0.099609375, 1.8984375).astype(jnp.bfloat16)
    q_weight = bell_draw(splits[3], (D, HEADS * HEAD_DIM), D ** -0.5, 0.1875, ((0, 32),))
    k_weight = bell_draw(splits[4], (D, KV_HEADS * HEAD_DIM), D ** -0.5, 0.1875, ((0, 32),))
    v_weight = bell_draw(splits[5], (D, KV_HEADS * HEAD_DIM), D ** -0.5, 0.1875, ((0, 32),))
    attn_gate_weight = bell_draw(splits[6], (D, HEADS), D ** -0.5, 0.1875, ((0, 32),))
    q_norm_gain = jnp.clip(jnp.exp(math.log(2.0) - 1.3862944 * jax.random.uniform(splits[7], (HEAD_DIM,), jnp.float32) ** levels(splits[7], (HEAD_DIM,), ((0, 32),), -0.2, 0.2)), 0.5, 2.0).astype(jnp.bfloat16)
    k_norm_gain = jnp.clip(jnp.exp(math.log(2.0) - 1.3862944 * jax.random.uniform(splits[8], (HEAD_DIM,), jnp.float32) ** levels(splits[8], (HEAD_DIM,), ((0, 32),), -0.2, 0.2)), 0.5, 2.0).astype(jnp.bfloat16)
    o_weight = bell_draw(splits[9], (HEADS * HEAD_DIM, D), 1 ** -0.5, 6.0, ((0, 32),))
    ln2_gain = jnp.clip(1.0 + 0.18 * jax.random.normal(splits[10], (D,), jnp.float32), 0.099609375, 1.8984375).astype(jnp.bfloat16)
    gate_weight = bell_draw(splits[11], (D, FF), D ** -0.5, 0.1875, ((0, 32),))
    up_weight = bell_draw(splits[12], (D, FF), D ** -0.5, 0.1875, ((0, 32),))
    down_weight = bell_draw(splits[13], (FF, D), FF ** -0.5, 0.109375, ((0, 32),))
    cotangent = heavy_noise(splits[14], (N_DP, GROUP_TOK, D), 1.0, 8.0, ((0, 4), (1, 8)), (1, 2, 8, 2.0))
    return dict(tokens=tokens, lengths=lengths, ln1_gain=ln1_gain, q_weight=q_weight, k_weight=k_weight, v_weight=v_weight, attn_gate_weight=attn_gate_weight, q_norm_gain=q_norm_gain, k_norm_gain=k_norm_gain, o_weight=o_weight, ln2_gain=ln2_gain, gate_weight=gate_weight, up_weight=up_weight, down_weight=down_weight, cotangent=cotangent)


EPS = 1e-06
THETA = 1000000.0
NEG = -1e+30

@jax.custom_vjp
def low(v):
    return lax.optimization_barrier(v.astype(jnp.bfloat16)).astype(jnp.float32)

@jax.custom_vjp
def low_back(v):
    return v

def low_keep(v):
    return (low(v), None)

def low_pass(kept, grad):
    return (grad,)

def back_keep(v):
    return (v, None)

def back_low(kept, grad):
    return (low(grad),)
low.defvjp(low_keep, low_pass)
low_back.defvjp(back_keep, back_low)

def matmul(left_op, right_op):
    return jnp.dot(left_op, right_op, precision=lax.Precision.HIGHEST)

def rms_rows(values_in):
    return values_in * lax.rsqrt(lax.optimization_barrier(jnp.mean(values_in * values_in, axis=-1, keepdims=True)) + EPS)

def token_info(lengths_row, first_tok, num_rows):
    seq_ends = jnp.cumsum(lengths_row).astype(jnp.int32)
    starts = (seq_ends - lengths_row).astype(jnp.int32)
    tok_index = first_tok + jnp.arange(num_rows, dtype=jnp.int32)
    segment = lax.optimization_barrier(jnp.sum((tok_index[:, None] >= seq_ends[None, :]).astype(jnp.int32), axis=1)).astype(jnp.int32)
    chosen = segment[:, None] == jnp.arange(lengths_row.shape[0], dtype=jnp.int32)[None, :]
    seq_begin = lax.optimization_barrier(jnp.sum(jnp.where(chosen, starts[None, :], 0), axis=1)).astype(jnp.int32)
    return (segment, (tok_index - seq_begin).astype(jnp.int32))

def rope_tables(position, width):
    half_width = width // 2
    inv_freq = THETA ** (-2.0 * jnp.arange(half_width, dtype=jnp.float32) / width)
    angles = position.astype(jnp.float32)[:, None] * inv_freq[None, :]
    cos_tab = jnp.concatenate([jnp.cos(angles), jnp.cos(angles)], axis=1)
    sin_tab = jnp.concatenate([jnp.sin(angles), jnp.sin(angles)], axis=1)
    return (cos_tab, sin_tab)

def rotate(shaped, cos_tab, sin_tab):
    half_width = shaped.shape[-1] // 2
    turned = jnp.concatenate([-shaped[..., half_width:], shaped[..., :half_width]], axis=-1)
    return shaped * cos_tab[:, None, :] + turned * sin_tab[:, None, :]

def head_prepare(raw_proj, gain_vec, cos_tab, sin_tab, head_count):
    shaped = raw_proj.reshape(raw_proj.shape[0], head_count, -1)
    return rotate(rms_rows(shaped) * gain_vec, cos_tab, sin_tab)

def attention(queries, key_rot, values, segment, block_id):
    tokens_n = queries.shape[0]
    size_q = math.gcd(tokens_n, 256)
    blocks_n = tokens_n // size_q
    rep_count = HEADS // KV_HEADS
    score_scale = 1.0 / math.sqrt(HEAD_DIM)
    query_blocks = queries.reshape(blocks_n, size_q, KV_HEADS, rep_count, HEAD_DIM)

    def one_block(query_part, seg_part, blk_part, keys_all, values_all, seg_all, blk_all):
        scores = jnp.einsum('tgrd,sgd->tgrs', query_part, keys_all, precision=lax.Precision.HIGHEST)
        scores = low_back(scores * score_scale)
        allowed = ((seg_part[:, None] == seg_all[None, :]) & (blk_all[None, :] <= blk_part[:, None]))[:, None, None, :]
        masked = jnp.where(allowed, scores, NEG)
        row_top = lax.optimization_barrier(jnp.max(masked, axis=3, keepdims=True))
        expo_vals = jnp.where(allowed, jnp.exp(masked - row_top), 0.0)
        prob_vals = low(expo_vals / lax.optimization_barrier(jnp.sum(expo_vals, axis=3, keepdims=True)))
        return jnp.einsum('tgrs,sgd->tgrd', prob_vals, values_all, precision=lax.Precision.HIGHEST)
    checked = jax.checkpoint(one_block)

    def per_block(block_items):
        return checked(block_items[0], block_items[1], block_items[2], key_rot, values, segment, block_id)
    result = lax.map(per_block, (query_blocks, segment.reshape(blocks_n, size_q), block_id.reshape(blocks_n, size_q)))
    return result.reshape(tokens_n, HEADS, HEAD_DIM)

def layer_forward(inputs, lengths_row, ln1_gain, q_weight, k_weight, v_weight, attn_gate_weight, q_norm_gain, k_norm_gain, o_weight, ln2_gain, gate_weight, up_weight, down_weight):
    tokens_n = inputs.shape[0]
    segment, position = token_info(lengths_row, 0, tokens_n)
    block_id = (position // BLOCK).astype(jnp.int32)
    cos_tab, sin_tab = rope_tables(position, HEAD_DIM)
    normed = low(rms_rows(inputs) * ln1_gain)
    q_raw = low_back(matmul(normed, q_weight))
    k_raw = low_back(matmul(normed, k_weight))
    values = low(low_back(matmul(normed, v_weight))).reshape(tokens_n, KV_HEADS, HEAD_DIM)
    gate_vals = jax.nn.sigmoid(low_back(matmul(normed, attn_gate_weight)))
    queries = low(head_prepare(q_raw, q_norm_gain, cos_tab, sin_tab, HEADS))
    key_rot = low(head_prepare(k_raw, k_norm_gain, cos_tab, sin_tab, KV_HEADS))
    attended = low_back(attention(queries, key_rot, values, segment, block_id))
    gated = low((attended * gate_vals[:, :, None]).reshape(tokens_n, -1))
    hidden_sum = inputs + low_back(matmul(gated, o_weight))
    normed_two = low(rms_rows(hidden_sum) * ln2_gain)
    gate_pre = low_back(matmul(normed_two, gate_weight))
    up_pre = low_back(matmul(normed_two, up_weight))
    activated = low(jax.nn.silu(gate_pre) * up_pre)
    return hidden_sum + low_back(matmul(activated, down_weight))

def reference(tokens, lengths, ln1_gain, q_weight, k_weight, v_weight, attn_gate_weight, q_norm_gain, k_norm_gain, o_weight, ln2_gain, gate_weight, up_weight, down_weight, cotangent):
    weights = tuple((weight_arr.astype(jnp.float32) for weight_arr in (ln1_gain, q_weight, k_weight, v_weight, attn_gate_weight, q_norm_gain, k_norm_gain, o_weight, ln2_gain, gate_weight, up_weight, down_weight)))
    grads_total = tuple((jnp.zeros_like(weight_arr) for weight_arr in weights))
    outputs = []
    input_grads = []
    for group_id in range(tokens.shape[0]):
        lengths_row = lengths[group_id]

        def group_fn(inputs, *params):
            return layer_forward(inputs, lengths_row, *params)
        result, pull_back = jax.vjp(group_fn, tokens[group_id].astype(jnp.float32), *weights)
        grad_list = pull_back(cotangent[group_id].astype(jnp.float32))
        outputs.append(result.astype(jnp.bfloat16))
        input_grads.append(grad_list[0])
        grads_total = tuple((total_one + grad_one for total_one, grad_one in zip(grads_total, grad_list[1:])))
    return (jnp.stack(outputs), jnp.stack(input_grads), grads_total[0], grads_total[1], grads_total[2], grads_total[3], grads_total[4], grads_total[5], grads_total[6], grads_total[7], grads_total[8], grads_total[9], grads_total[10], grads_total[11])
```

```python
from functools import partial
import math

import jax
import jax.numpy as jnp
from jax import lax
from jax.sharding import PartitionSpec as P

HEADS = 16
KV_HEADS = 8
HEAD_DIM = 128
BLOCK = 256


EPS = 1e-06
THETA = 1000000.0
NEG = -1e30


def matmul(left_op, right_op):
    return jnp.dot(left_op, right_op, preferred_element_type=jnp.float32)


def matmul_nt(left_op, right_op):
    return lax.dot_general(
        left_op, right_op, (((1,), (1,)), ((), ())), preferred_element_type=jnp.float32
    )


def matmul_tn(left_op, right_op):
    return lax.dot_general(
        left_op, right_op, (((0,), (0,)), ((), ())), preferred_element_type=jnp.float32
    )


def rms_rows(values_in):
    return values_in * lax.rsqrt(jnp.mean(values_in * values_in, axis=-1, keepdims=True) + EPS)


def gained_norm(values_in, gain_vec):
    return rms_rows(values_in) * gain_vec


def swiglu(gate_in, up_in):
    return jax.nn.silu(gate_in) * up_in


def token_info(lengths_row, first_tok, num_rows):
    seq_ends = jnp.cumsum(lengths_row)
    starts = seq_ends - lengths_row
    tok_index = first_tok + jnp.arange(num_rows, dtype=jnp.int32)
    segment = jnp.sum((tok_index[:, None] >= seq_ends[None, :]).astype(jnp.int32), axis=1)
    chosen = segment[:, None] == jnp.arange(lengths_row.shape[0], dtype=jnp.int32)[None, :]
    seq_begin = jnp.sum(jnp.where(chosen, starts[None, :], 0), axis=1)
    return (segment, tok_index - seq_begin)


def rope_tables(position, width):
    half_width = width // 2
    inv_freq = THETA ** (-2.0 * jnp.arange(half_width, dtype=jnp.float32) / width)
    angles = position.astype(jnp.float32)[:, None] * inv_freq[None, :]
    cos_tab = jnp.concatenate([jnp.cos(angles), jnp.cos(angles)], axis=1)
    sin_tab = jnp.concatenate([jnp.sin(angles), jnp.sin(angles)], axis=1)
    return (cos_tab, sin_tab)


def rotate(shaped, cos_tab, sin_tab):
    half_width = shaped.shape[-1] // 2
    turned = jnp.concatenate([-shaped[..., half_width:], shaped[..., :half_width]], axis=-1)
    return shaped * cos_tab[:, None, :] + turned * sin_tab[:, None, :]


def head_prepare(raw_proj, gain_vec, cos_tab, sin_tab, head_count):
    shaped = raw_proj.reshape(raw_proj.shape[0], head_count, -1)
    return rotate(rms_rows(shaped) * gain_vec, cos_tab, sin_tab)


def keep_running(running, *others):
    return running


def by_blocks(step_fn, running, pieces, offset):
    num_keys = pieces[0].shape[0]
    if num_keys <= 1024 or num_keys % 512 != 0:
        return step_fn(running, pieces, offset)
    number = num_keys // 512
    split_parts = tuple(
        (one_part.reshape((number, 512) + one_part.shape[1:]) for one_part in pieces)
    )

    def advance(current, scan_item):
        blocks, block_pos = scan_item
        return (step_fn(current, blocks, offset + block_pos * 512), None)

    result, unused_out = lax.scan(
        advance, running, (split_parts, jnp.arange(number, dtype=jnp.int32))
    )
    return result


def gathered_layer(
    tokens,
    lengths,
    ln1_gain,
    q_weight,
    k_weight,
    v_weight,
    attn_gate_weight,
    q_norm_gain,
    k_norm_gain,
    o_weight,
    ln2_gain,
    gate_weight,
    up_weight,
    down_weight,
    cotangent,
):
    inputs = tokens[0].astype(jnp.float32)
    num_rows = inputs.shape[0]
    seq_devices = lax.axis_size("seq")
    lengths_row = lengths[0]
    seg_query, pos_query = token_info(lengths_row, lax.axis_index("seq") * num_rows, num_rows)
    blk_query = pos_query // BLOCK
    cos_tab, sin_tab = rope_tables(pos_query, HEAD_DIM)
    rep_count = HEADS // KV_HEADS
    score_scale = 1.0 / math.sqrt(HEAD_DIM)
    attn_full = (
        lax.all_gather(ln1_gain, ("seq", "dp"), axis=0, tiled=True),
        lax.all_gather(q_weight, ("seq", "dp"), axis=0, tiled=True),
        lax.all_gather(k_weight, ("seq", "dp"), axis=0, tiled=True),
        lax.all_gather(v_weight, ("seq", "dp"), axis=0, tiled=True),
        lax.all_gather(attn_gate_weight, ("seq", "dp"), axis=0, tiled=True),
        lax.all_gather(q_norm_gain, ("seq", "dp"), axis=0, tiled=True),
        lax.all_gather(k_norm_gain, ("seq", "dp"), axis=0, tiled=True),
        lax.all_gather(o_weight, ("seq", "dp"), axis=0, tiled=True),
    )
    ln1_vec = attn_full[0].astype(jnp.float32)
    q_gain = attn_full[5].astype(jnp.float32)
    k_gain = attn_full[6].astype(jnp.float32)
    normed_b = gained_norm(inputs, ln1_vec).astype(jnp.bfloat16)
    q_raw = matmul(normed_b, attn_full[1])
    k_raw = matmul(normed_b, attn_full[2])
    values_b = (
        matmul(normed_b, attn_full[3]).astype(jnp.bfloat16).reshape(num_rows, KV_HEADS, HEAD_DIM)
    )
    gate_vals = jax.nn.sigmoid(matmul(normed_b, attn_full[4]))
    queries_b = head_prepare(q_raw, q_gain, cos_tab, sin_tab, HEADS).astype(jnp.bfloat16)
    keys_b = head_prepare(k_raw, k_gain, cos_tab, sin_tab, KV_HEADS).astype(jnp.bfloat16)
    query_grp = queries_b.reshape(num_rows, KV_HEADS, rep_count, HEAD_DIM)
    lead_shape = (num_rows, KV_HEADS, rep_count)

    def mask_for(offset, num_keys):
        seg_key, pos_key = token_info(lengths_row, offset, num_keys)
        return (seg_query[:, None] == seg_key[None, :]) & (
            (pos_key // BLOCK)[None, :] <= blk_query[:, None]
        )

    def forward_update(running, pieces, allowed):
        run_max, weight_sum, out_accum = running
        key_part, value_part = pieces
        mask_full = allowed[:, None, None, :]
        scores = (
            jnp.einsum("tgrd,sgd->tgrs", query_grp, key_part, preferred_element_type=jnp.float32)
            * score_scale
        )
        masked = jnp.where(mask_full, scores, NEG)
        new_max = jnp.maximum(run_max, jnp.max(masked, axis=3))
        weights = jnp.where(mask_full, jnp.exp(masked - new_max[..., None]), 0.0)
        factor = jnp.exp(run_max - new_max)
        weight_sum = weight_sum * factor + jnp.sum(weights, axis=3)
        out_accum = out_accum * factor[..., None] + jnp.einsum(
            "tgrs,sgd->tgrd",
            weights.astype(jnp.bfloat16),
            value_part,
            preferred_element_type=jnp.float32,
        )
        return (new_max, weight_sum, out_accum)

    def forward_step(running, pieces, offset):
        allowed = mask_for(offset, pieces[0].shape[0])
        return lax.cond(jnp.any(allowed), forward_update, keep_running, running, pieces, allowed)

    start_state = (
        jnp.full(lead_shape, NEG, jnp.float32),
        jnp.zeros(lead_shape, jnp.float32),
        jnp.zeros(lead_shape + (HEAD_DIM,), jnp.float32),
    )
    run_max, weight_sum, out_accum = by_blocks(
        forward_step,
        start_state,
        (
            lax.all_gather(keys_b, "seq", axis=0, tiled=True),
            lax.all_gather(values_b, "seq", axis=0, tiled=True),
        ),
        jnp.int32(0),
    )
    attended = (out_accum / weight_sum[..., None]).reshape(num_rows, HEADS, HEAD_DIM)
    log_sums = run_max + jnp.log(weight_sum)
    gated_b = (attended * gate_vals[:, :, None]).reshape(num_rows, -1).astype(jnp.bfloat16)
    hidden_sum = inputs + matmul(gated_b, attn_full[7])
    mlp_full = (
        lax.all_gather(ln2_gain, ("seq", "dp"), axis=0, tiled=True),
        lax.all_gather(gate_weight, ("seq", "dp"), axis=0, tiled=True),
        lax.all_gather(up_weight, ("seq", "dp"), axis=0, tiled=True),
        lax.all_gather(down_weight, ("seq", "dp"), axis=0, tiled=True),
    )
    ln2_vec = mlp_full[0].astype(jnp.float32)
    normed_two_b = gained_norm(hidden_sum, ln2_vec).astype(jnp.bfloat16)
    gate_pre = matmul(normed_two_b, mlp_full[1])
    up_pre = matmul(normed_two_b, mlp_full[2])
    activated_b = swiglu(gate_pre, up_pre).astype(jnp.bfloat16)
    layer_out = (hidden_sum + matmul(activated_b, mlp_full[3])).astype(jnp.bfloat16)
    mlp_back = (
        lax.all_gather(gate_weight, ("seq", "dp"), axis=0, tiled=True),
        lax.all_gather(up_weight, ("seq", "dp"), axis=0, tiled=True),
        lax.all_gather(down_weight, ("seq", "dp"), axis=0, tiled=True),
    )
    grad_out_b = cotangent[0]
    grad_act = matmul_nt(grad_out_b, mlp_back[2])
    unused_act, swiglu_pull = jax.vjp(swiglu, gate_pre, up_pre)
    grad_gate_pre, grad_up_pre = swiglu_pull(grad_act)
    grad_gate_b = grad_gate_pre.astype(jnp.bfloat16)
    grad_up_b = grad_up_pre.astype(jnp.bfloat16)
    grad_normed_two = matmul_nt(grad_gate_b, mlp_back[0]) + matmul_nt(grad_up_b, mlp_back[1])
    unused_two, norm_two_pull = jax.vjp(gained_norm, hidden_sum, ln2_vec)
    grad_hidden_part, ln2_term = norm_two_pull(grad_normed_two)
    grad_hidden = grad_out_b.astype(jnp.float32) + grad_hidden_part
    down_term = matmul_tn(activated_b, grad_out_b)
    gate_term = matmul_tn(normed_two_b, grad_gate_b)
    up_term = matmul_tn(normed_two_b, grad_up_b)
    mlp_grads = (
        lax.psum_scatter(ln2_term, ("seq", "dp"), scatter_dimension=0, tiled=True),
        lax.psum_scatter(gate_term, ("seq", "dp"), scatter_dimension=0, tiled=True),
        lax.psum_scatter(up_term, ("seq", "dp"), scatter_dimension=0, tiled=True),
        lax.psum_scatter(down_term, ("seq", "dp"), scatter_dimension=0, tiled=True),
    )
    attn_back = (
        lax.all_gather(q_weight, ("seq", "dp"), axis=0, tiled=True),
        lax.all_gather(k_weight, ("seq", "dp"), axis=0, tiled=True),
        lax.all_gather(v_weight, ("seq", "dp"), axis=0, tiled=True),
        lax.all_gather(attn_gate_weight, ("seq", "dp"), axis=0, tiled=True),
        lax.all_gather(o_weight, ("seq", "dp"), axis=0, tiled=True),
    )
    grad_hidden_b = grad_hidden.astype(jnp.bfloat16)
    o_term = matmul_tn(gated_b, grad_hidden_b)
    grad_gated = matmul_nt(grad_hidden_b, attn_back[4]).reshape(num_rows, HEADS, HEAD_DIM)
    grad_gate_vals = jnp.sum(grad_gated * attended, axis=2)
    grad_logit_b = (grad_gate_vals * gate_vals * (1.0 - gate_vals)).astype(jnp.bfloat16)
    grad_attended_b = (grad_gated * gate_vals[:, :, None]).astype(jnp.bfloat16)
    row_delta = jnp.sum(grad_attended_b.astype(jnp.float32) * attended, axis=2).reshape(lead_shape)
    dout_grp = grad_attended_b.reshape(num_rows, KV_HEADS, rep_count, HEAD_DIM)

    def backward_update(running, pieces, allowed, offset):
        grad_query, grad_kv_all = running
        key_part, value_part = pieces
        num_keys = key_part.shape[0]
        mask_full = allowed[:, None, None, :]
        scores = (
            jnp.einsum("tgrd,sgd->tgrs", query_grp, key_part, preferred_element_type=jnp.float32)
            * score_scale
        )
        prob_vals = jnp.where(mask_full, jnp.exp(scores - log_sums[..., None]), 0.0)
        grad_prob = jnp.einsum(
            "tgrd,sgd->tgrs", dout_grp, value_part, preferred_element_type=jnp.float32
        )
        grad_score_b = (prob_vals * (grad_prob - row_delta[..., None])).astype(jnp.bfloat16)
        grad_query = (
            grad_query
            + jnp.einsum(
                "tgrs,sgd->tgrd", grad_score_b, key_part, preferred_element_type=jnp.float32
            )
            * score_scale
        )
        grad_key = (
            jnp.einsum(
                "tgrs,tgrd->sgd", grad_score_b, query_grp, preferred_element_type=jnp.float32
            )
            * score_scale
        )
        grad_value = jnp.einsum(
            "tgrs,tgrd->sgd",
            prob_vals.astype(jnp.bfloat16),
            dout_grp,
            preferred_element_type=jnp.float32,
        )
        kv_block = jnp.concatenate(
            [grad_key.reshape(num_keys, -1), grad_value.reshape(num_keys, -1)], axis=1
        )
        grad_kv_all = lax.dynamic_update_slice_in_dim(grad_kv_all, kv_block, offset, 0)
        return (grad_query, grad_kv_all)

    def backward_step(running, pieces, offset):
        allowed = mask_for(offset, pieces[0].shape[0])
        return lax.cond(
            jnp.any(allowed), backward_update, keep_running, running, pieces, allowed, offset
        )

    back_state = (
        jnp.zeros(lead_shape + (HEAD_DIM,), jnp.float32),
        jnp.zeros((num_rows * seq_devices, 2 * KV_HEADS * HEAD_DIM), jnp.float32),
    )
    grad_query, grad_kv_all = by_blocks(
        backward_step,
        back_state,
        (
            lax.all_gather(keys_b, "seq", axis=0, tiled=True),
            lax.all_gather(values_b, "seq", axis=0, tiled=True),
        ),
        jnp.int32(0),
    )
    grad_kv = lax.psum_scatter(
        grad_kv_all.astype(jnp.bfloat16), "seq", scatter_dimension=0, tiled=True
    ).astype(jnp.float32)
    half_cols = KV_HEADS * HEAD_DIM
    grad_key_rot = grad_kv[:, :half_cols].reshape(num_rows, KV_HEADS, HEAD_DIM)
    grad_values_b = grad_kv[:, half_cols:].astype(jnp.bfloat16)
    unused_q, q_pull = jax.vjp(
        partial(head_prepare, cos_tab=cos_tab, sin_tab=sin_tab, head_count=HEADS), q_raw, q_gain
    )
    grad_q_raw, qn_term = q_pull(grad_query.reshape(num_rows, HEADS, HEAD_DIM))
    unused_k, k_pull = jax.vjp(
        partial(head_prepare, cos_tab=cos_tab, sin_tab=sin_tab, head_count=KV_HEADS), k_raw, k_gain
    )
    grad_k_raw, kn_term = k_pull(grad_key_rot)
    grad_q_b = grad_q_raw.astype(jnp.bfloat16)
    grad_k_b = grad_k_raw.astype(jnp.bfloat16)
    q_term = matmul_tn(normed_b, grad_q_b)
    k_term = matmul_tn(normed_b, grad_k_b)
    v_term = matmul_tn(normed_b, grad_values_b)
    logit_term = matmul_tn(normed_b, grad_logit_b)
    grad_normed = (
        matmul_nt(grad_q_b, attn_back[0])
        + matmul_nt(grad_k_b, attn_back[1])
        + matmul_nt(grad_values_b, attn_back[2])
        + matmul_nt(grad_logit_b, attn_back[3])
    )
    unused_one, norm_one_pull = jax.vjp(gained_norm, inputs, ln1_vec)
    grad_input_part, ln1_term = norm_one_pull(grad_normed)
    grad_input = grad_hidden + grad_input_part
    attn_grads = (
        lax.psum_scatter(ln1_term, ("seq", "dp"), scatter_dimension=0, tiled=True),
        lax.psum_scatter(q_term, ("seq", "dp"), scatter_dimension=0, tiled=True),
        lax.psum_scatter(k_term, ("seq", "dp"), scatter_dimension=0, tiled=True),
        lax.psum_scatter(v_term, ("seq", "dp"), scatter_dimension=0, tiled=True),
        lax.psum_scatter(logit_term, ("seq", "dp"), scatter_dimension=0, tiled=True),
        lax.psum_scatter(qn_term, ("seq", "dp"), scatter_dimension=0, tiled=True),
        lax.psum_scatter(kn_term, ("seq", "dp"), scatter_dimension=0, tiled=True),
        lax.psum_scatter(o_term, ("seq", "dp"), scatter_dimension=0, tiled=True),
    )
    return (
        layer_out[None],
        grad_input[None],
        attn_grads[0],
        attn_grads[1],
        attn_grads[2],
        attn_grads[3],
        attn_grads[4],
        attn_grads[5],
        attn_grads[6],
        attn_grads[7],
        mlp_grads[0],
        mlp_grads[1],
        mlp_grads[2],
        mlp_grads[3],
    )


def tensor_parallel_layer(
    tokens,
    lengths,
    ln1_gain,
    q_weight,
    k_weight,
    v_weight,
    attn_gate_weight,
    q_norm_gain,
    k_norm_gain,
    o_weight,
    ln2_gain,
    gate_weight,
    up_weight,
    down_weight,
    cotangent,
):
    bf16, f32 = jnp.bfloat16, jnp.float32
    seq_at, plane = lax.axis_index("seq"), lax.axis_index("dp")
    chip, core = seq_at // 2, seq_at % 2
    block = tokens.shape[1]
    own_rows = 4 * block
    heads, kv_heads = HEADS // 4, KV_HEADS // 4
    rep_count = HEADS // KV_HEADS
    score_scale = 1.0 / math.sqrt(HEAD_DIM)
    q_cols, kv_cols = heads * HEAD_DIM, kv_heads * HEAD_DIM
    ff_cols = gate_weight.shape[1] // 4
    model = tokens.shape[2]
    gain_rows = q_norm_gain.shape[0]

    def to_chip(value, k):
        return lax.ppermute(value, "seq", [(s, s ^ (2 * k)) for s in range(8)])

    def to_core(value):
        return lax.ppermute(value, "seq", [(s, s ^ 1) for s in range(8)])

    def to_plane(value, e):
        return lax.ppermute(value, "dp", [(d, d ^ e) for d in range(4)])

    def chip_gather(value):
        return [value] + [to_chip(value, k) for k in (1, 2, 3)]

    def chip_scatter(pieces):
        total = pieces[0].astype(f32)
        for k in (1, 2, 3):
            total = total + to_chip(pieces[k].astype(bf16), k).astype(f32)
        return total

    def gather_rows(value):
        pieces = jnp.stack([value] + [to_plane(value, e) for e in (1, 2, 3)])
        return jnp.stack([pieces, to_core(pieces)])

    def row_parallel(weight):
        rows = weight.shape[0]
        both = gather_rows(weight).reshape(8, rows, -1)
        order = jnp.arange(8, dtype=jnp.int32) ^ (core * 4 + plane)
        return both[order].reshape(8 * rows, -1)

    def column_parallel(slices):
        rows = slices(0).shape[0]
        swapped = jnp.stack([slices(chip)] + [to_chip(slices(chip ^ k), k) for k in (1, 2, 3)])
        both = gather_rows(swapped)
        both = both.reshape(32, rows, -1)
        at = jnp.arange(32, dtype=jnp.int32)
        source = (((at // 4) % 2) ^ core) * 16 + ((at % 4) ^ plane) * 4 + ((at // 8) ^ chip)
        return both[source].reshape(32 * rows, -1)

    def take(value, at, size):
        return lax.dynamic_slice_in_dim(value, at * size, size, 1)

    def qkv_slice(j):
        small = jnp.concatenate(
            [
                take(attn_gate_weight, j, heads),
                ln1_gain[:, None],
                ln2_gain[:, None],
                jnp.pad(q_norm_gain, (0, ln1_gain.shape[0] - gain_rows))[:, None],
                jnp.pad(k_norm_gain, (0, ln1_gain.shape[0] - gain_rows))[:, None],
            ],
            axis=1,
        )
        small = jnp.pad(small, ((0, 0), (0, 128 - small.shape[1])))
        return jnp.concatenate(
            [take(q_weight, j, q_cols), take(k_weight, j, kv_cols), take(v_weight, j, kv_cols), small],
            axis=1,
        )

    def ff_slice(j):
        return jnp.concatenate([take(gate_weight, j, ff_cols), take(up_weight, j, ff_cols)], axis=1)

    qkv_w = column_parallel(qkv_slice)
    inputs = jnp.concatenate(chip_gather(tokens[0]), axis=0).astype(f32)
    split_at = (q_cols, q_cols + kv_cols, q_cols + 2 * kv_cols)
    q_w, k_w, v_w, small_w = jnp.split(qkv_w, split_at, axis=1)
    logit_w = small_w[:, :heads]
    ln1_vec = small_w[:, heads].astype(f32)
    ln2_vec = small_w[:, heads + 1].astype(f32)
    q_gain = small_w[:, heads + 2].reshape(32, -1)[:, :gain_rows].reshape(-1).astype(f32)
    k_gain = small_w[:, heads + 3].reshape(32, -1)[:, :gain_rows].reshape(-1).astype(f32)

    o_w = row_parallel(o_weight)
    ff_w = column_parallel(ff_slice)
    down_w = row_parallel(down_weight)
    grad_out = jnp.concatenate(chip_gather(cotangent[0]), axis=0)

    lengths_row = lengths[0]
    seq_ends = jnp.cumsum(lengths_row)
    starts = seq_ends - lengths_row

    def place(core_at):
        slot = jnp.arange(4, dtype=jnp.int32) ^ chip
        index = ((2 * slot + core_at) * block)[:, None] + jnp.arange(block, dtype=jnp.int32)[None, :]
        index = index.reshape(-1)
        segment = jnp.sum((index[:, None] >= seq_ends[None, :]).astype(jnp.int32), axis=1)
        chosen = segment[:, None] == jnp.arange(lengths_row.shape[0], dtype=jnp.int32)[None, :]
        return segment, index - jnp.sum(jnp.where(chosen, starts[None, :], 0), axis=1)

    seg_query, pos_query = place(core)
    seg_other, pos_other = place(1 - core)
    seg_key = jnp.concatenate([seg_query, seg_other])
    blk_key = jnp.concatenate([pos_query, pos_other]) // BLOCK
    allowed = (seg_query[:, None] == seg_key[None, :]) & (
        blk_key[None, :] <= (pos_query // BLOCK)[:, None]
    )
    cos_tab, sin_tab = rope_tables(pos_query, HEAD_DIM)

    normed_b = gained_norm(inputs, ln1_vec).astype(bf16)
    q_raw = matmul(normed_b, q_w)
    k_raw = matmul(normed_b, k_w)
    values_b = matmul(normed_b, v_w).astype(bf16)
    gate_vals = jax.nn.sigmoid(matmul(normed_b, logit_w))
    queries_b = head_prepare(q_raw, q_gain, cos_tab, sin_tab, heads).astype(bf16)
    keys_b = head_prepare(k_raw, k_gain, cos_tab, sin_tab, kv_heads).astype(bf16)
    own_kv = jnp.concatenate([keys_b.reshape(own_rows, -1), values_b], axis=1)
    all_kv = jnp.concatenate([own_kv, to_core(own_kv)], axis=0)
    key_all = all_kv[:, :kv_cols].reshape(2 * own_rows, kv_heads, HEAD_DIM)
    value_all = all_kv[:, kv_cols:].reshape(2 * own_rows, kv_heads, HEAD_DIM)
    query_grp = queries_b.reshape(own_rows, kv_heads, rep_count, HEAD_DIM)

    mask_full = allowed[None, None]
    scores = (
        jnp.einsum("tgrd,sgd->grts", query_grp, key_all, preferred_element_type=f32) * score_scale
    )
    masked = jnp.where(mask_full, scores, NEG)
    row_max = jnp.max(masked, axis=3, keepdims=True)
    expo = jnp.exp(masked - row_max)
    weight_sum = jnp.sum(expo, axis=3, keepdims=True)
    log_sums = row_max + jnp.log(weight_sum)
    prob_b = (expo / weight_sum).astype(bf16)
    attended = jnp.einsum("grts,sgd->tgrd", prob_b, value_all, preferred_element_type=f32)
    attended = attended.reshape(own_rows, heads, HEAD_DIM)
    gated_b = (attended * gate_vals[:, :, None]).reshape(own_rows, -1).astype(bf16)
    o_part = matmul(gated_b, o_w).astype(bf16).reshape(4, block, model)
    hidden_own = tokens[0].astype(f32) + chip_scatter(o_part)
    normed_two_own = gained_norm(hidden_own, ln2_vec).astype(bf16)
    normed_two_b = jnp.concatenate(chip_gather(normed_two_own), axis=0)
    gate_pre = matmul(normed_two_b, ff_w[:, :ff_cols])
    up_pre = matmul(normed_two_b, ff_w[:, ff_cols:])
    activated_b = swiglu(gate_pre, up_pre).astype(bf16)

    grad_act = matmul_nt(grad_out, down_w)
    unused_act, swiglu_pull = jax.vjp(swiglu, gate_pre, up_pre)
    grad_gate_pre, grad_up_pre = swiglu_pull(grad_act)
    grad_ff_b = jnp.concatenate([grad_gate_pre.astype(bf16), grad_up_pre.astype(bf16)], axis=1)
    two_part = matmul_nt(grad_ff_b, ff_w).astype(bf16).reshape(4, block, model)
    grad_normed_two = chip_scatter(two_part)
    unused_two, norm_two_pull = jax.vjp(gained_norm, hidden_own, ln2_vec)
    grad_hidden_part, ln2_term = norm_two_pull(grad_normed_two)
    grad_hidden = cotangent[0].astype(f32) + grad_hidden_part
    grad_hidden_b = jnp.concatenate(chip_gather(grad_hidden.astype(bf16)), axis=0)
    out_part = matmul(activated_b, down_w).astype(bf16).reshape(4, block, model)
    layer_out = (hidden_own + chip_scatter(out_part)).astype(bf16)

    def reduce_rows(term, lead, rows):
        width = term.shape[1]
        cut = term.reshape(lead, 2, 4, rows, width)
        sent = lax.dynamic_index_in_dim(cut, 1 - core, 1, keepdims=False).astype(bf16)
        kept = lax.dynamic_index_in_dim(cut, core, 1, keepdims=False)
        half = (kept + to_core(sent).astype(f32)).astype(bf16)
        total = lax.dynamic_index_in_dim(half, plane, 1, keepdims=False).astype(f32)
        for e in (1, 2, 3):
            piece = lax.dynamic_index_in_dim(half, plane ^ e, 1, keepdims=False)
            total = total + to_plane(piece, e).astype(f32)
        return total

    def reduce_columns(term, rows):
        total = reduce_rows(term, 4, rows).astype(bf16)
        pieces = [
            lax.dynamic_index_in_dim(total, chip ^ k, 0, keepdims=False) for k in range(4)
        ]
        got = [pieces[0]] + [to_chip(pieces[k], k) for k in (1, 2, 3)]
        stacked = jnp.stack(got)
        return stacked[jnp.arange(4, dtype=jnp.int32) ^ chip]

    def spread(pieces):
        return jnp.concatenate([pieces[j] for j in range(4)], axis=1).astype(f32)

    down_grad = reduce_rows(matmul_tn(activated_b, grad_out), 1, down_weight.shape[0])[0]
    ff_pieces = reduce_columns(matmul_tn(normed_two_b, grad_ff_b), gate_weight.shape[0])
    gate_grad = spread(ff_pieces[:, :, :ff_cols])
    up_grad = spread(ff_pieces[:, :, ff_cols:])

    o_grad = reduce_rows(matmul_tn(gated_b, grad_hidden_b), 1, o_weight.shape[0])[0]
    grad_gated = matmul_nt(grad_hidden_b, o_w).reshape(own_rows, heads, HEAD_DIM)
    grad_gate_vals = jnp.sum(grad_gated * attended, axis=2)
    grad_logit_b = (grad_gate_vals * gate_vals * (1.0 - gate_vals)).astype(bf16)
    grad_attended_b = (grad_gated * gate_vals[:, :, None]).astype(bf16)
    row_delta = jnp.sum(grad_attended_b.astype(f32) * attended, axis=2)
    row_delta = row_delta.reshape(own_rows, kv_heads, rep_count).transpose(1, 2, 0)[..., None]
    dout_grp = grad_attended_b.reshape(own_rows, kv_heads, rep_count, HEAD_DIM)
    scores_two = (
        jnp.einsum("tgrd,sgd->grts", query_grp, key_all, preferred_element_type=f32) * score_scale
    )
    prob_vals = jnp.where(mask_full, jnp.exp(scores_two - log_sums), 0.0)
    grad_prob = jnp.einsum("tgrd,sgd->grts", dout_grp, value_all, preferred_element_type=f32)
    grad_score_b = (prob_vals * (grad_prob - row_delta)).astype(bf16)
    grad_query = (
        jnp.einsum("grts,sgd->tgrd", grad_score_b, key_all, preferred_element_type=f32)
        * score_scale
    )
    grad_key = (
        jnp.einsum("grts,tgrd->sgd", grad_score_b, query_grp, preferred_element_type=f32)
        * score_scale
    )
    grad_value = jnp.einsum(
        "grts,tgrd->sgd", prob_vals.astype(bf16), dout_grp, preferred_element_type=f32
    )
    grad_kv = jnp.concatenate(
        [grad_key.reshape(2 * own_rows, -1), grad_value.reshape(2 * own_rows, -1)], axis=1
    )
    grad_kv = grad_kv[:own_rows] + to_core(grad_kv[own_rows:].astype(bf16)).astype(f32)
    unused_q, q_pull = jax.vjp(
        partial(head_prepare, cos_tab=cos_tab, sin_tab=sin_tab, head_count=heads), q_raw, q_gain
    )
    grad_q_raw, qn_term = q_pull(grad_query.reshape(own_rows, heads, HEAD_DIM))
    unused_k, k_pull = jax.vjp(
        partial(head_prepare, cos_tab=cos_tab, sin_tab=sin_tab, head_count=kv_heads), k_raw, k_gain
    )
    grad_k_raw, kn_term = k_pull(grad_kv[:, :kv_cols].reshape(own_rows, kv_heads, HEAD_DIM))
    grad_qkv_b = jnp.concatenate(
        [grad_q_raw.astype(bf16), grad_k_raw.astype(bf16), grad_kv[:, kv_cols:].astype(bf16)], axis=1
    )
    one_part = matmul_nt(grad_qkv_b, qkv_w[:, : q_cols + 2 * kv_cols]) + matmul_nt(
        grad_logit_b, logit_w
    )
    unit = rms_rows(inputs)
    ln1_term = jnp.sum(one_part * unit, axis=0)
    qkv_term = matmul_tn(normed_b, grad_qkv_b)
    logit_term = matmul_tn(normed_b, grad_logit_b)

    def short_column(vector):
        return jnp.pad(vector.reshape(32, gain_rows), ((0, 0), (0, model // 32 - gain_rows))).reshape(-1, 1)

    small_term = jnp.concatenate(
        [logit_term, ln1_term[:, None], ln2_term[:, None], short_column(qn_term), short_column(kn_term)],
        axis=1,
    )
    small_term = jnp.pad(small_term, ((0, 0), (0, 128 - small_term.shape[1])))
    qkv_pieces = reduce_columns(jnp.concatenate([qkv_term, small_term], axis=1), q_weight.shape[0])
    q_grad = spread(qkv_pieces[:, :, :q_cols])
    k_grad = spread(qkv_pieces[:, :, split_at[0] : split_at[1]])
    v_grad = spread(qkv_pieces[:, :, split_at[1] : split_at[2]])
    small_pieces = qkv_pieces[:, :, split_at[2] :].astype(f32)
    logit_grad = spread(small_pieces[:, :, :heads])
    sums = jnp.sum(small_pieces, axis=0)
    ln1_grad = sums[:, heads]
    ln2_grad = sums[:, heads + 1]
    qn_grad = sums[:gain_rows, heads + 2]
    kn_grad = sums[:gain_rows, heads + 3]

    grad_normed = chip_scatter(one_part.astype(bf16).reshape(4, block, model))
    inputs_own = tokens[0].astype(f32)
    unused_one, norm_one_pull = jax.vjp(gained_norm, inputs_own, ln1_vec)
    grad_input_part, unused_term = norm_one_pull(grad_normed)
    grad_input = grad_hidden + grad_input_part
    return (
        layer_out[None],
        grad_input[None],
        ln1_grad,
        q_grad,
        k_grad,
        v_grad,
        logit_grad,
        qn_grad,
        kn_grad,
        o_grad,
        ln2_grad,
        gate_grad,
        up_grad,
        down_grad,
    )


def solution(mesh):
    split_heads = mesh.shape["seq"] == 8 and mesh.shape["dp"] == 4
    in_specs = (
        P("dp", "seq", None),
        P("dp", None),
        P(("seq", "dp")),
        P(("seq", "dp"), None),
        P(("seq", "dp"), None),
        P(("seq", "dp"), None),
        P(("seq", "dp"), None),
        P(("seq", "dp")),
        P(("seq", "dp")),
        P(("seq", "dp"), None),
        P(("seq", "dp")),
        P(("seq", "dp"), None),
        P(("seq", "dp"), None),
        P(("seq", "dp"), None),
        P("dp", "seq", None),
    )
    out_specs = (
        P("dp", "seq", None),
        P("dp", "seq", None),
        P(("seq", "dp")),
        P(("seq", "dp"), None),
        P(("seq", "dp"), None),
        P(("seq", "dp"), None),
        P(("seq", "dp"), None),
        P(("seq", "dp")),
        P(("seq", "dp")),
        P(("seq", "dp"), None),
        P(("seq", "dp")),
        P(("seq", "dp"), None),
        P(("seq", "dp"), None),
        P(("seq", "dp"), None),
    )
    return jax.shard_map(
        tensor_parallel_layer if split_heads else gathered_layer,
        mesh=mesh, in_specs=in_specs, out_specs=out_specs, check_vma=False
    )
```

```python
from functools import partial
import math

import jax
import jax.numpy as jnp
from jax import lax
from jax.experimental import pallas as pl
from jax.experimental.pallas import tpu as pltpu
from jax.sharding import PartitionSpec as P

HEADS = 16
KV_HEADS = 8
HEAD_DIM = 128
BLOCK = 256


EPS = 1e-06
THETA = 1000000.0
NEG = -1e30


def matmul(left_op, right_op):
    return jnp.dot(left_op, right_op, preferred_element_type=jnp.float32)


def matmul_nt(left_op, right_op):
    return lax.dot_general(
        left_op, right_op, (((1,), (1,)), ((), ())), preferred_element_type=jnp.float32
    )


def matmul_tn(left_op, right_op):
    return lax.dot_general(
        left_op, right_op, (((0,), (0,)), ((), ())), preferred_element_type=jnp.float32
    )


def rms_rows(values_in):
    return values_in * lax.rsqrt(jnp.mean(values_in * values_in, axis=-1, keepdims=True) + EPS)


def gained_norm(values_in, gain_vec):
    return rms_rows(values_in) * gain_vec


def swiglu(gate_in, up_in):
    return jax.nn.silu(gate_in) * up_in


def token_info(lengths_row, first_tok, num_rows):
    seq_ends = jnp.cumsum(lengths_row)
    starts = seq_ends - lengths_row
    tok_index = first_tok + jnp.arange(num_rows, dtype=jnp.int32)
    segment = jnp.sum((tok_index[:, None] >= seq_ends[None, :]).astype(jnp.int32), axis=1)
    chosen = segment[:, None] == jnp.arange(lengths_row.shape[0], dtype=jnp.int32)[None, :]
    seq_begin = jnp.sum(jnp.where(chosen, starts[None, :], 0), axis=1)
    return (segment, tok_index - seq_begin)


def rope_tables(position, width):
    half_width = width // 2
    inv_freq = THETA ** (-2.0 * jnp.arange(half_width, dtype=jnp.float32) / width)
    angles = position.astype(jnp.float32)[:, None] * inv_freq[None, :]
    cos_tab = jnp.concatenate([jnp.cos(angles), jnp.cos(angles)], axis=1)
    sin_tab = jnp.concatenate([jnp.sin(angles), jnp.sin(angles)], axis=1)
    return (cos_tab, sin_tab)


def rotate(shaped, cos_tab, sin_tab):
    half_width = shaped.shape[-1] // 2
    turned = jnp.concatenate([-shaped[..., half_width:], shaped[..., :half_width]], axis=-1)
    return shaped * cos_tab[:, None, :] + turned * sin_tab[:, None, :]


def head_prepare(raw_proj, gain_vec, cos_tab, sin_tab, head_count):
    shaped = raw_proj.reshape(raw_proj.shape[0], head_count, -1)
    return rotate(rms_rows(shaped) * gain_vec, cos_tab, sin_tab)


def keep_running(running, *others):
    return running


def by_blocks(step_fn, running, pieces, offset):
    num_keys = pieces[0].shape[0]
    if num_keys <= 1024 or num_keys % 512 != 0:
        return step_fn(running, pieces, offset)
    number = num_keys // 512
    split_parts = tuple(
        (one_part.reshape((number, 512) + one_part.shape[1:]) for one_part in pieces)
    )

    def advance(current, scan_item):
        blocks, block_pos = scan_item
        return (step_fn(current, blocks, offset + block_pos * 512), None)

    result, unused_out = lax.scan(
        advance, running, (split_parts, jnp.arange(number, dtype=jnp.int32))
    )
    return result


def gathered_layer(
    tokens,
    lengths,
    ln1_gain,
    q_weight,
    k_weight,
    v_weight,
    attn_gate_weight,
    q_norm_gain,
    k_norm_gain,
    o_weight,
    ln2_gain,
    gate_weight,
    up_weight,
    down_weight,
    cotangent,
):
    inputs = tokens[0].astype(jnp.float32)
    num_rows = inputs.shape[0]
    seq_devices = lax.axis_size("seq")
    lengths_row = lengths[0]
    seg_query, pos_query = token_info(lengths_row, lax.axis_index("seq") * num_rows, num_rows)
    blk_query = pos_query // BLOCK
    cos_tab, sin_tab = rope_tables(pos_query, HEAD_DIM)
    rep_count = HEADS // KV_HEADS
    score_scale = 1.0 / math.sqrt(HEAD_DIM)
    attn_full = (
        lax.all_gather(ln1_gain, ("seq", "dp"), axis=0, tiled=True),
        lax.all_gather(q_weight, ("seq", "dp"), axis=0, tiled=True),
        lax.all_gather(k_weight, ("seq", "dp"), axis=0, tiled=True),
        lax.all_gather(v_weight, ("seq", "dp"), axis=0, tiled=True),
        lax.all_gather(attn_gate_weight, ("seq", "dp"), axis=0, tiled=True),
        lax.all_gather(q_norm_gain, ("seq", "dp"), axis=0, tiled=True),
        lax.all_gather(k_norm_gain, ("seq", "dp"), axis=0, tiled=True),
        lax.all_gather(o_weight, ("seq", "dp"), axis=0, tiled=True),
    )
    ln1_vec = attn_full[0].astype(jnp.float32)
    q_gain = attn_full[5].astype(jnp.float32)
    k_gain = attn_full[6].astype(jnp.float32)
    normed_b = gained_norm(inputs, ln1_vec).astype(jnp.bfloat16)
    q_raw = matmul(normed_b, attn_full[1])
    k_raw = matmul(normed_b, attn_full[2])
    values_b = (
        matmul(normed_b, attn_full[3]).astype(jnp.bfloat16).reshape(num_rows, KV_HEADS, HEAD_DIM)
    )
    gate_vals = jax.nn.sigmoid(matmul(normed_b, attn_full[4]))
    queries_b = head_prepare(q_raw, q_gain, cos_tab, sin_tab, HEADS).astype(jnp.bfloat16)
    keys_b = head_prepare(k_raw, k_gain, cos_tab, sin_tab, KV_HEADS).astype(jnp.bfloat16)
    query_grp = queries_b.reshape(num_rows, KV_HEADS, rep_count, HEAD_DIM)
    lead_shape = (num_rows, KV_HEADS, rep_count)

    def mask_for(offset, num_keys):
        seg_key, pos_key = token_info(lengths_row, offset, num_keys)
        return (seg_query[:, None] == seg_key[None, :]) & (
            (pos_key // BLOCK)[None, :] <= blk_query[:, None]
        )

    def forward_update(running, pieces, allowed):
        run_max, weight_sum, out_accum = running
        key_part, value_part = pieces
        mask_full = allowed[:, None, None, :]
        scores = (
            jnp.einsum("tgrd,sgd->tgrs", query_grp, key_part, preferred_element_type=jnp.float32)
            * score_scale
        )
        masked = jnp.where(mask_full, scores, NEG)
        new_max = jnp.maximum(run_max, jnp.max(masked, axis=3))
        weights = jnp.where(mask_full, jnp.exp(masked - new_max[..., None]), 0.0)
        factor = jnp.exp(run_max - new_max)
        weight_sum = weight_sum * factor + jnp.sum(weights, axis=3)
        out_accum = out_accum * factor[..., None] + jnp.einsum(
            "tgrs,sgd->tgrd",
            weights.astype(jnp.bfloat16),
            value_part,
            preferred_element_type=jnp.float32,
        )
        return (new_max, weight_sum, out_accum)

    def forward_step(running, pieces, offset):
        allowed = mask_for(offset, pieces[0].shape[0])
        return lax.cond(jnp.any(allowed), forward_update, keep_running, running, pieces, allowed)

    start_state = (
        jnp.full(lead_shape, NEG, jnp.float32),
        jnp.zeros(lead_shape, jnp.float32),
        jnp.zeros(lead_shape + (HEAD_DIM,), jnp.float32),
    )
    run_max, weight_sum, out_accum = by_blocks(
        forward_step,
        start_state,
        (
            lax.all_gather(keys_b, "seq", axis=0, tiled=True),
            lax.all_gather(values_b, "seq", axis=0, tiled=True),
        ),
        jnp.int32(0),
    )
    attended = (out_accum / weight_sum[..., None]).reshape(num_rows, HEADS, HEAD_DIM)
    log_sums = run_max + jnp.log(weight_sum)
    gated_b = (attended * gate_vals[:, :, None]).reshape(num_rows, -1).astype(jnp.bfloat16)
    hidden_sum = inputs + matmul(gated_b, attn_full[7])
    mlp_full = (
        lax.all_gather(ln2_gain, ("seq", "dp"), axis=0, tiled=True),
        lax.all_gather(gate_weight, ("seq", "dp"), axis=0, tiled=True),
        lax.all_gather(up_weight, ("seq", "dp"), axis=0, tiled=True),
        lax.all_gather(down_weight, ("seq", "dp"), axis=0, tiled=True),
    )
    ln2_vec = mlp_full[0].astype(jnp.float32)
    normed_two_b = gained_norm(hidden_sum, ln2_vec).astype(jnp.bfloat16)
    gate_pre = matmul(normed_two_b, mlp_full[1])
    up_pre = matmul(normed_two_b, mlp_full[2])
    activated_b = swiglu(gate_pre, up_pre).astype(jnp.bfloat16)
    layer_out = (hidden_sum + matmul(activated_b, mlp_full[3])).astype(jnp.bfloat16)
    mlp_back = (
        lax.all_gather(gate_weight, ("seq", "dp"), axis=0, tiled=True),
        lax.all_gather(up_weight, ("seq", "dp"), axis=0, tiled=True),
        lax.all_gather(down_weight, ("seq", "dp"), axis=0, tiled=True),
    )
    grad_out_b = cotangent[0]
    grad_act = matmul_nt(grad_out_b, mlp_back[2])
    unused_act, swiglu_pull = jax.vjp(swiglu, gate_pre, up_pre)
    grad_gate_pre, grad_up_pre = swiglu_pull(grad_act)
    grad_gate_b = grad_gate_pre.astype(jnp.bfloat16)
    grad_up_b = grad_up_pre.astype(jnp.bfloat16)
    grad_normed_two = matmul_nt(grad_gate_b, mlp_back[0]) + matmul_nt(grad_up_b, mlp_back[1])
    unused_two, norm_two_pull = jax.vjp(gained_norm, hidden_sum, ln2_vec)
    grad_hidden_part, ln2_term = norm_two_pull(grad_normed_two)
    grad_hidden = grad_out_b.astype(jnp.float32) + grad_hidden_part
    down_term = matmul_tn(activated_b, grad_out_b)
    gate_term = matmul_tn(normed_two_b, grad_gate_b)
    up_term = matmul_tn(normed_two_b, grad_up_b)
    mlp_grads = (
        lax.psum_scatter(ln2_term, ("seq", "dp"), scatter_dimension=0, tiled=True),
        lax.psum_scatter(gate_term, ("seq", "dp"), scatter_dimension=0, tiled=True),
        lax.psum_scatter(up_term, ("seq", "dp"), scatter_dimension=0, tiled=True),
        lax.psum_scatter(down_term, ("seq", "dp"), scatter_dimension=0, tiled=True),
    )
    attn_back = (
        lax.all_gather(q_weight, ("seq", "dp"), axis=0, tiled=True),
        lax.all_gather(k_weight, ("seq", "dp"), axis=0, tiled=True),
        lax.all_gather(v_weight, ("seq", "dp"), axis=0, tiled=True),
        lax.all_gather(attn_gate_weight, ("seq", "dp"), axis=0, tiled=True),
        lax.all_gather(o_weight, ("seq", "dp"), axis=0, tiled=True),
    )
    grad_hidden_b = grad_hidden.astype(jnp.bfloat16)
    o_term = matmul_tn(gated_b, grad_hidden_b)
    grad_gated = matmul_nt(grad_hidden_b, attn_back[4]).reshape(num_rows, HEADS, HEAD_DIM)
    grad_gate_vals = jnp.sum(grad_gated * attended, axis=2)
    grad_logit_b = (grad_gate_vals * gate_vals * (1.0 - gate_vals)).astype(jnp.bfloat16)
    grad_attended_b = (grad_gated * gate_vals[:, :, None]).astype(jnp.bfloat16)
    row_delta = jnp.sum(grad_attended_b.astype(jnp.float32) * attended, axis=2).reshape(lead_shape)
    dout_grp = grad_attended_b.reshape(num_rows, KV_HEADS, rep_count, HEAD_DIM)

    def backward_update(running, pieces, allowed, offset):
        grad_query, grad_kv_all = running
        key_part, value_part = pieces
        num_keys = key_part.shape[0]
        mask_full = allowed[:, None, None, :]
        scores = (
            jnp.einsum("tgrd,sgd->tgrs", query_grp, key_part, preferred_element_type=jnp.float32)
            * score_scale
        )
        prob_vals = jnp.where(mask_full, jnp.exp(scores - log_sums[..., None]), 0.0)
        grad_prob = jnp.einsum(
            "tgrd,sgd->tgrs", dout_grp, value_part, preferred_element_type=jnp.float32
        )
        grad_score_b = (prob_vals * (grad_prob - row_delta[..., None])).astype(jnp.bfloat16)
        grad_query = (
            grad_query
            + jnp.einsum(
                "tgrs,sgd->tgrd", grad_score_b, key_part, preferred_element_type=jnp.float32
            )
            * score_scale
        )
        grad_key = (
            jnp.einsum(
                "tgrs,tgrd->sgd", grad_score_b, query_grp, preferred_element_type=jnp.float32
            )
            * score_scale
        )
        grad_value = jnp.einsum(
            "tgrs,tgrd->sgd",
            prob_vals.astype(jnp.bfloat16),
            dout_grp,
            preferred_element_type=jnp.float32,
        )
        kv_block = jnp.concatenate(
            [grad_key.reshape(num_keys, -1), grad_value.reshape(num_keys, -1)], axis=1
        )
        grad_kv_all = lax.dynamic_update_slice_in_dim(grad_kv_all, kv_block, offset, 0)
        return (grad_query, grad_kv_all)

    def backward_step(running, pieces, offset):
        allowed = mask_for(offset, pieces[0].shape[0])
        return lax.cond(
            jnp.any(allowed), backward_update, keep_running, running, pieces, allowed, offset
        )

    back_state = (
        jnp.zeros(lead_shape + (HEAD_DIM,), jnp.float32),
        jnp.zeros((num_rows * seq_devices, 2 * KV_HEADS * HEAD_DIM), jnp.float32),
    )
    grad_query, grad_kv_all = by_blocks(
        backward_step,
        back_state,
        (
            lax.all_gather(keys_b, "seq", axis=0, tiled=True),
            lax.all_gather(values_b, "seq", axis=0, tiled=True),
        ),
        jnp.int32(0),
    )
    grad_kv = lax.psum_scatter(
        grad_kv_all.astype(jnp.bfloat16), "seq", scatter_dimension=0, tiled=True
    ).astype(jnp.float32)
    half_cols = KV_HEADS * HEAD_DIM
    grad_key_rot = grad_kv[:, :half_cols].reshape(num_rows, KV_HEADS, HEAD_DIM)
    grad_values_b = grad_kv[:, half_cols:].astype(jnp.bfloat16)
    unused_q, q_pull = jax.vjp(
        partial(head_prepare, cos_tab=cos_tab, sin_tab=sin_tab, head_count=HEADS), q_raw, q_gain
    )
    grad_q_raw, qn_term = q_pull(grad_query.reshape(num_rows, HEADS, HEAD_DIM))
    unused_k, k_pull = jax.vjp(
        partial(head_prepare, cos_tab=cos_tab, sin_tab=sin_tab, head_count=KV_HEADS), k_raw, k_gain
    )
    grad_k_raw, kn_term = k_pull(grad_key_rot)
    grad_q_b = grad_q_raw.astype(jnp.bfloat16)
    grad_k_b = grad_k_raw.astype(jnp.bfloat16)
    q_term = matmul_tn(normed_b, grad_q_b)
    k_term = matmul_tn(normed_b, grad_k_b)
    v_term = matmul_tn(normed_b, grad_values_b)
    logit_term = matmul_tn(normed_b, grad_logit_b)
    grad_normed = (
        matmul_nt(grad_q_b, attn_back[0])
        + matmul_nt(grad_k_b, attn_back[1])
        + matmul_nt(grad_values_b, attn_back[2])
        + matmul_nt(grad_logit_b, attn_back[3])
    )
    unused_one, norm_one_pull = jax.vjp(gained_norm, inputs, ln1_vec)
    grad_input_part, ln1_term = norm_one_pull(grad_normed)
    grad_input = grad_hidden + grad_input_part
    attn_grads = (
        lax.psum_scatter(ln1_term, ("seq", "dp"), scatter_dimension=0, tiled=True),
        lax.psum_scatter(q_term, ("seq", "dp"), scatter_dimension=0, tiled=True),
        lax.psum_scatter(k_term, ("seq", "dp"), scatter_dimension=0, tiled=True),
        lax.psum_scatter(v_term, ("seq", "dp"), scatter_dimension=0, tiled=True),
        lax.psum_scatter(logit_term, ("seq", "dp"), scatter_dimension=0, tiled=True),
        lax.psum_scatter(qn_term, ("seq", "dp"), scatter_dimension=0, tiled=True),
        lax.psum_scatter(kn_term, ("seq", "dp"), scatter_dimension=0, tiled=True),
        lax.psum_scatter(o_term, ("seq", "dp"), scatter_dimension=0, tiled=True),
    )
    return (
        layer_out[None],
        grad_input[None],
        attn_grads[0],
        attn_grads[1],
        attn_grads[2],
        attn_grads[3],
        attn_grads[4],
        attn_grads[5],
        attn_grads[6],
        attn_grads[7],
        mlp_grads[0],
        mlp_grads[1],
        mlp_grads[2],
        mlp_grads[3],
    )


bf16, f32 = jnp.bfloat16, jnp.float32
LANE = 128
LN1_AT, LN2_AT, QN_AT, KN_AT = HEADS, HEADS + 1, HEADS + 2, HEADS + 3
LOG2E = 1.4426950408889634


def iota(shape, axis):
    return lax.broadcasted_iota(jnp.int32, shape, axis)


def aligned(at, size):
    return pl.ds(pl.multiple_of(at * size, size), size)


def column_of(row):
    count = row.shape[1]
    square = (count, count)
    return jnp.sum(jnp.where(iota(square, 0) == iota(square, 1), row, 0.0), axis=1, keepdims=True)


def row_of(column):
    count = column.shape[0]
    square = (count, count)
    return jnp.sum(jnp.where(iota(square, 0) == iota(square, 1), column, 0.0), axis=0, keepdims=True)


def short_places(model):
    shape = (model, HEAD_DIM)
    per_block, rows = HEAD_DIM // 32, model // 32
    block, inner = iota(shape, 0) // rows, iota(shape, 0) % rows
    entry = iota(shape, 1)
    return (entry // per_block == block) & (entry % per_block == inner)


def on_core(body, name, ids, args, outs, scratch=(), copies=0, scalars=1):
    vmem, smem = pl.BlockSpec(memory_space=pltpu.VMEM), pl.BlockSpec(memory_space=pltpu.SMEM)
    source = pl.BlockSpec(memory_space=pltpu.HBM) if copies else vmem
    shapes = [pltpu.VMEM(shape, kind) for shape, kind in scratch]
    if copies:
        shapes.append(pltpu.SemaphoreType.DMA((copies,)))
    return pl.pallas_call(
        body,
        name=name,
        out_shape=[jax.ShapeDtypeStruct(shape, kind) for shape, kind in outs],
        in_specs=[smem] * scalars + [source] * (1 + len(args) - scalars),
        out_specs=[vmem] * len(outs),
        scratch_shapes=shapes,
        compiler_params=pltpu.CompilerParams(vmem_limit_bytes=14 * 1024 * 1024),
    )(ids, *args)


def run_copies(pairs, sems):
    copies = [pltpu.make_async_copy(src, dst, sems.at[at]) for at, (src, dst) in enumerate(pairs)]
    for copy in copies:
        copy.start()
    for copy in copies:
        copy.wait()


def pack_attention(ids, q_ref, k_ref, v_ref, logit_ref, ln1_ref, ln2_ref, qn_ref, kn_ref, *refs):
    outs, (logit_own, ln1_own, ln2_own, qn_own, kn_own, sems) = refs[:4], refs[4:]
    rows = q_ref.shape[0]
    q_cols, kv_cols = q_ref.shape[1] // 4, k_ref.shape[1] // 4
    pairs = [
        (logit_ref, logit_own),
        (ln1_ref, ln1_own),
        (ln2_ref, ln2_own),
        (qn_ref, qn_own),
        (kn_ref, kn_own),
    ]
    for k, out in enumerate(outs):
        chip = ids[0] ^ k
        pairs += [
            (q_ref.at[:, aligned(chip, q_cols)], out.at[:, :q_cols]),
            (k_ref.at[:, aligned(chip, kv_cols)], out.at[:, q_cols : q_cols + kv_cols]),
            (v_ref.at[:, aligned(chip, kv_cols)], out.at[:, q_cols + kv_cols : q_cols + 2 * kv_cols]),
        ]
    run_copies(pairs, sems)
    lane = iota((rows, LANE), 1)
    small = jnp.zeros((rows, LANE), f32)
    for at, ref in ((LN1_AT, ln1_own), (LN2_AT, ln2_own), (QN_AT, qn_own), (KN_AT, kn_own)):
        row = ref[...].astype(f32)
        shape = (rows, row.shape[1])
        column = jnp.sum(
            jnp.where(iota(shape, 0) == iota(shape, 1), row, 0.0), axis=1, keepdims=True
        )
        small = jnp.where(lane == at, column, small)
    small = small.astype(bf16)
    for out in outs:
        out[:, q_cols + 2 * kv_cols :] = small
        out[:, q_cols + 2 * kv_cols : q_cols + 2 * kv_cols + HEADS] = logit_own[...]


def pack_forward(ids, gate_ref, up_ref, *refs):
    outs, sems = refs[:4], refs[4]
    cols = gate_ref.shape[1] // 4
    pairs = []
    for k, out in enumerate(outs):
        pairs += [
            (gate_ref.at[:, aligned(ids[0] ^ k, cols)], out.at[:, :cols]),
            (up_ref.at[:, aligned(ids[0] ^ k, cols)], out.at[:, cols:]),
        ]
    run_copies(pairs, sems)


def join_four(ids, *refs):
    for k in range(4):
        refs[4][k] = refs[k][...]


def positions(ids, lengths_ref, cos_out, sin_out, code_out, limit_out):
    rows = cos_out.shape[0]
    block = rows // 4

    def place(index):
        segment, begin, end = jnp.zeros_like(index), jnp.zeros_like(index), 0
        for at in range(lengths_ref.shape[1]):
            end = end + lengths_ref[0, at]
            passed = index >= end
            segment += jnp.where(passed, 1, 0)
            begin = jnp.where(passed, end, begin)
        return segment, index - begin

    def token(row, core):
        return (2 * ((row // block) ^ ids[0]) + core) * block + row % block

    column = iota((rows, 1), 0)
    segment, position = place(token(column, ids[1]))
    code_out[:rows, :] = segment * rows + position // BLOCK
    other_segment, other_position = place(token(column, 1 - ids[1]))
    code_out[rows:, :] = other_segment * rows + other_position // BLOCK
    row_segment, row_position = place(token(iota((1, rows), 1), ids[1]))
    limit_out[...] = jnp.zeros(limit_out.shape, jnp.int32)
    limit_out[0:1, :] = row_segment * rows
    limit_out[1:2, :] = row_segment * rows + row_position // BLOCK
    lane = iota((1, HEAD_DIM), 1)
    half = HEAD_DIM // 2
    rate = jnp.exp((lane % half).astype(f32) * (-2.0 * math.log(THETA) / HEAD_DIM))
    angles = position.astype(f32) * rate
    cos_out[...] = jnp.cos(angles)
    sin_out[...] = jnp.sin(angles) * jnp.where(lane < half, -1.0, 1.0)


def place_columns(ids, pieces, out):
    for f in range(2):
        for e in range(4):
            for k in range(4):
                rows = pieces[4 * f + e].shape[1]
                at = 8 * (ids[0] ^ k) + 4 * (ids[1] ^ f) + (ids[2] ^ e)
                out[aligned(at, rows), :] = pieces[4 * f + e][k]


def place_rows(ids, pieces, out):
    for f in range(2):
        for e in range(4):
            rows = pieces[4 * f + e].shape[0]
            at = 4 * (ids[1] ^ f) + (ids[2] ^ e)
            out[aligned(at, rows), :] = pieces[4 * f + e][...]


def head_rotate(value, cos, sin):
    return value * cos + pltpu.roll(value, HEAD_DIM // 2, 1) * sin


def project(ids, *refs):
    tokens, pieces, tables = refs[:4], refs[4:12], refs[12:14]
    w_out, normed_out, raw_out, q_out, kv_out, gate_out, rows_out = refs[14:]
    block, model = tokens[0].shape
    q_cols = q_out.shape[1]
    kv_cols = kv_out.shape[1] // 2
    place_columns(ids, pieces, w_out)
    small = w_out[:, q_cols + 2 * kv_cols :].astype(f32)
    turned = jnp.transpose(small)
    rows_out[...] = jnp.zeros(rows_out.shape, f32)
    rows_out[0:1, :] = turned[LN1_AT : LN1_AT + 1, :]
    rows_out[1:2, :] = turned[LN2_AT : LN2_AT + 1, :]
    places = short_places(model)
    for at, source in ((2, QN_AT), (3, KN_AT)):
        column = small[:, source : source + 1]
        rows_out[at : at + 1, :HEAD_DIM] = jnp.sum(
            jnp.where(places, column, 0.0), axis=0, keepdims=True
        )
    gain = rows_out[0:1, :]
    for k in range(4):
        values = tokens[k][...].astype(f32)
        normed_out[k * block : (k + 1) * block, :] = (rms_rows(values) * gain).astype(bf16)
    raw_out[...] = matmul(normed_out[...], w_out[:, : q_cols + kv_cols])
    kv_out[:, kv_cols:] = matmul(
        normed_out[...], w_out[:, q_cols + kv_cols : q_cols + 2 * kv_cols]
    ).astype(bf16)
    gate_out[...] = jax.nn.sigmoid(matmul(normed_out[...], w_out[:, q_cols + 2 * kv_cols :]))
    cos, sin = tables[0][...], tables[1][...]
    for head in range((q_cols + kv_cols) // HEAD_DIM):
        cols = slice(head * HEAD_DIM, (head + 1) * HEAD_DIM)
        is_query = head * HEAD_DIM < q_cols
        head_gain = rows_out[2:3, :HEAD_DIM] if is_query else rows_out[3:4, :HEAD_DIM]
        turned_head = head_rotate(rms_rows(raw_out[:, cols]) * head_gain, cos, sin).astype(bf16)
        if is_query:
            q_out[:, cols] = turned_head
        else:
            kv_out[:, head * HEAD_DIM - q_cols : (head + 1) * HEAD_DIM - q_cols] = turned_head


def head_gate(gates, ids, head, heads):
    lane = iota(gates.shape, 1)
    return jnp.sum(jnp.where(lane == ids[0] * heads + head, gates, 0.0), axis=1, keepdims=True)


def attend(ids, q_ref, own_ref, other_ref, gate_ref, code_ref, limit_ref, *refs):
    pieces = refs[:8]
    parts, (attended_out, gated_out, lse_out, o_out) = refs[8:12], refs[12:16]
    kt_ref, total_ref, sum_ref = refs[16:]
    rows = q_ref.shape[0]
    heads = q_ref.shape[1] // HEAD_DIM
    kv_heads = own_ref.shape[1] // (2 * HEAD_DIM)
    rep_count = heads // kv_heads
    chunk = 256
    place_rows(ids, pieces, o_out)
    total_ref[...] = jnp.zeros(total_ref.shape, f32)
    sum_ref[...] = jnp.zeros(sum_ref.shape, f32)
    low, high = limit_ref[0:1, :], limit_ref[1:2, :]
    for half, kv_ref in enumerate((own_ref, other_ref)):
        for group in range(kv_heads):
            cols = slice((kv_heads + group) * HEAD_DIM, (kv_heads + group + 1) * HEAD_DIM)
            kt_ref[group, :, half * rows : (half + 1) * rows] = jnp.transpose(kv_ref[:, cols])
    for half, kv_ref in enumerate((own_ref, other_ref)):

        def one_chunk(at, carry):
            place = half * rows + at * chunk
            code = code_ref[pl.ds(pl.multiple_of(place, chunk), chunk), :]
            allowed = (code >= low) & (code <= high)
            for head in range(heads):
                group = head // rep_count
                keys = kv_ref[aligned(at, chunk), group * HEAD_DIM : (group + 1) * HEAD_DIM]
                scores = matmul_nt(keys, q_ref[:, head * HEAD_DIM : (head + 1) * HEAD_DIM])
                expo = jnp.where(
                    allowed, jnp.exp2(scores * (LOG2E / math.sqrt(HEAD_DIM))), 0.0
                )
                sum_ref[head : head + 1, :] += jnp.sum(expo, axis=0, keepdims=True)
                total_ref[head] += matmul(
                    kt_ref[group, :, pl.ds(pl.multiple_of(place, chunk), chunk)],
                    expo.astype(bf16),
                )
            return carry

        lax.fori_loop(0, rows // chunk, one_chunk, 0)
    lse_out[...] = jnp.log2(sum_ref[...])
    gates = gate_ref[...]
    for head in range(heads):
        cols = slice(head * HEAD_DIM, (head + 1) * HEAD_DIM)
        out = jnp.transpose(total_ref[head] * (1.0 / sum_ref[head : head + 1, :]))
        attended_out[:, cols] = out
        gated_out[:, cols] = (out * head_gate(gates, ids, head, heads)).astype(bf16)
    block = parts[0].shape[0]
    for k, part in enumerate(parts):
        part[...] = matmul(gated_out[k * block : (k + 1) * block, :], o_out[...]).astype(bf16)


def four_sum(refs):
    return sum([ref[...].astype(f32) for ref in refs[1:]], refs[0][...].astype(f32))


def join_hidden(ids, tokens_ref, rows_ref, *refs):
    hidden = tokens_ref[...].astype(f32) + four_sum(refs[:4])
    refs[4][...] = hidden
    refs[5][...] = (rms_rows(hidden) * rows_ref[1:2, :]).astype(bf16)


def feed_forward(ids, *refs):
    normed, cots, ff_pieces, down_pieces = refs[:4], refs[4:8], refs[8:16], refs[16:24]
    parts, (act_out, grad_out, normed_out, cot_out, down_out), (w_ref,) = refs[24:28], refs[28:33], refs[33:]
    block = normed[0].shape[0]
    ff_cols = act_out.shape[1]
    place_columns(ids, ff_pieces, w_ref)
    place_rows(ids, down_pieces, down_out)
    for k in range(4):
        normed_out[k * block : (k + 1) * block, :] = normed[k][...]
        cot_out[k * block : (k + 1) * block, :] = cots[k][...]
    chunk = 256
    for at in range(ff_cols // chunk):
        cols = slice(at * chunk, (at + 1) * chunk)
        up_cols = slice(ff_cols + at * chunk, ff_cols + (at + 1) * chunk)
        gate_pre = matmul(normed_out[...], w_ref[:, cols])
        up_pre = matmul(normed_out[...], w_ref[:, up_cols])
        grad_act = matmul_nt(cot_out[...], down_out[cols, :])
        sig = jax.nn.sigmoid(gate_pre)
        silu = gate_pre * sig
        act_out[:, cols] = (silu * up_pre).astype(bf16)
        grad_out[:, cols] = (grad_act * up_pre * (sig * (1.0 + gate_pre * (1.0 - sig)))).astype(bf16)
        grad_out[:, up_cols] = (grad_act * silu).astype(bf16)
    for k, part in enumerate(parts):
        part[...] = matmul_nt(grad_out[k * block : (k + 1) * block, :], w_ref[...]).astype(bf16)


def forward_out(ids, act_ref, down_ref, *parts):
    block = parts[0].shape[0]
    for k, part in enumerate(parts):
        part[...] = matmul(act_ref[k * block : (k + 1) * block, :], down_ref[...]).astype(bf16)


def keep_or_send(ids, low, high, kept, sent):
    mine = ids[1] == 0
    kept[...] = jnp.where(mine, low, high).astype(bf16)
    sent[...] = jnp.where(mine, high, low).astype(bf16)


def forward_grads(ids, act_ref, grad_ref, normed_ref, cot_ref, *outs):
    ff_kept, ff_sent, down_kept, down_sent = outs[:4]
    (turned_ref, turned_act) = outs[4:]
    turned_ref[...] = jnp.transpose(normed_ref[...])
    turned_act[...] = jnp.transpose(act_ref[...])
    half = ff_kept.shape[1]
    for chip in range(4):
        rows = turned_ref[chip * 2 * half : (chip + 1) * 2 * half, :]
        term = matmul(rows, grad_ref[...])
        keep_or_send(ids, term[:half], term[half:], ff_kept.at[chip], ff_sent.at[chip])
    rows = down_kept.shape[0]
    chunk = 256
    for at in range(down_kept.shape[1] // chunk):
        cols = slice(at * chunk, (at + 1) * chunk)
        term = matmul(turned_act[...], cot_ref[:, cols])
        keep_or_send(ids, term[:rows], term[rows:], down_kept.at[:, cols], down_sent.at[:, cols])


def o_grads(ids, gated_ref, cot_ref, kept, sent, turned_ref):
    turned_ref[...] = jnp.transpose(gated_ref[...])
    rows = kept.shape[0]
    chunk = 256
    for at in range(kept.shape[1] // chunk):
        cols = slice(at * chunk, (at + 1) * chunk)
        term = matmul(turned_ref[...], cot_ref[:, cols])
        keep_or_send(ids, term[:rows], term[rows:], kept.at[:, cols], sent.at[:, cols])


def core_sum_columns(ids, kept, got, outs):
    rows = outs[0].shape[1]
    for e, out in enumerate(outs):
        for chip in range(4):
            at = aligned(ids[2] ^ e, rows)
            out[chip] = (kept[chip, at, :].astype(f32) + got[chip, at, :].astype(f32)).astype(bf16)


def core_sum_rows(ids, kept, got, outs):
    rows = outs[0].shape[0]
    for e, out in enumerate(outs):
        at = aligned(ids[2] ^ e, rows)
        out[...] = (kept[at, :].astype(f32) + got[at, :].astype(f32)).astype(bf16)


def core_sum_forward(ids, ff_kept, ff_got, down_kept, down_got, *outs):
    core_sum_columns(ids, ff_kept, ff_got, outs[:4])
    core_sum_rows(ids, down_kept, down_got, outs[4:])


def core_sum_one(ids, kept, got, *outs):
    (core_sum_columns if len(kept.shape) == 3 else core_sum_rows)(ids, kept, got, outs)


def pair_sum(ids, *refs):
    count = len(refs) // 3
    for at in range(count):
        refs[2 * count + at][...] = (
            refs[2 * at][...].astype(f32) + refs[2 * at + 1][...].astype(f32)
        ).astype(bf16)


def plane_sum_columns(ids, own, near, far, *outs):
    for k, out in enumerate(outs):
        chip = ids[0] ^ k
        out[...] = (
            own[chip].astype(f32) + near[chip].astype(f32) + far[chip].astype(f32)
        ).astype(bf16)


def plane_sum_rows(ids, own, near, far, out):
    out[...] = own[...].astype(f32) + near[...].astype(f32) + far[...].astype(f32)


def spread_forward(ids, *refs):
    pieces, (gate_out, up_out) = refs[:4], refs[4:]
    cols = gate_out.shape[1] // 4
    for k in range(4):
        gate_out[:, aligned(ids[0] ^ k, cols)] = pieces[k][:, :cols].astype(f32)
        up_out[:, aligned(ids[0] ^ k, cols)] = pieces[k][:, cols:].astype(f32)


def second_norm_back(ids, hidden_ref, cot_ref, rows_ref, *refs):
    grad = four_sum(refs[:4])
    hidden = hidden_ref[...]
    scale = lax.rsqrt(jnp.mean(hidden * hidden, axis=-1, keepdims=True) + EPS)
    unit = hidden * scale
    gained = grad * rows_ref[1:2, :]
    total = cot_ref[...].astype(f32) + scale * (
        gained - unit * jnp.mean(gained * unit, axis=-1, keepdims=True)
    )
    refs[4][...] = total
    refs[5][...] = total.astype(bf16)
    refs[6][...] = jnp.zeros(refs[6].shape, f32)
    refs[6][0:1, :] = jnp.sum(grad * unit, axis=0, keepdims=True)


def first_norm_back(ids, tokens_ref, hidden_grad_ref, rows_ref, *refs):
    grad = four_sum(refs[:4])
    values = tokens_ref[...].astype(f32)
    scale = lax.rsqrt(jnp.mean(values * values, axis=-1, keepdims=True) + EPS)
    unit = values * scale
    gained = grad * rows_ref[0:1, :]
    refs[4][...] = hidden_grad_ref[...] + scale * (
        gained - unit * jnp.mean(gained * unit, axis=-1, keepdims=True)
    )


def join_out(ids, hidden_ref, *refs):
    refs[4][...] = (hidden_ref[...] + four_sum(refs[:4])).astype(bf16)


def attend_back(ids, *refs):
    cots, (o_ref, attended_ref, gate_ref, q_ref, own_ref, other_ref, lse_ref, code_ref, limit_ref) = (
        refs[:4],
        refs[4:13],
    )
    dq_out, dkv_own, dkv_other, dlogit_out, cot_out = refs[13:18]
    do_ref, delta_ref, kt_ref, dqt_ref = refs[18:]
    rows, heads = q_ref.shape[0], q_ref.shape[1] // HEAD_DIM
    kv_heads = own_ref.shape[1] // (2 * HEAD_DIM)
    rep_count = heads // kv_heads
    block = cots[0].shape[0]
    scale = 1.0 / math.sqrt(HEAD_DIM)
    for k in range(4):
        cot_out[k * block : (k + 1) * block, :] = cots[k][...]
    gates = gate_ref[...]
    lane = iota(gates.shape, 1)
    dlogit = jnp.zeros(gates.shape, f32)
    delta_ref[...] = jnp.zeros(delta_ref.shape, f32)
    for head in range(heads):
        cols = slice(head * HEAD_DIM, (head + 1) * HEAD_DIM)
        grad = matmul_nt(cot_out[...], o_ref[cols, :])
        out = attended_ref[:, cols]
        gate = head_gate(gates, ids, head, heads)
        logit = jnp.sum(grad * out, axis=1, keepdims=True) * gate * (1.0 - gate)
        dlogit = jnp.where(lane == ids[0] * heads + head, logit, dlogit)
        do = (grad * gate).astype(bf16)
        do_ref[:, cols] = do
        delta_ref[head : head + 1, :] = jnp.sum(
            jnp.transpose(do.astype(f32) * out), axis=0, keepdims=True
        )
    dlogit_out[...] = dlogit.astype(bf16)
    dqt_ref[...] = jnp.zeros(dqt_ref.shape, f32)
    low, high = limit_ref[0:1, :], limit_ref[1:2, :]
    chunk = 256
    for half, kv_ref in enumerate((own_ref, other_ref)):
        for group in range(kv_heads):
            cols = slice(group * HEAD_DIM, (group + 1) * HEAD_DIM)
            kt_ref[group, :, half * rows : (half + 1) * rows] = jnp.transpose(kv_ref[:, cols])
    for half, (kv_ref, dkv_ref) in enumerate(((other_ref, dkv_other), (own_ref, dkv_own))):

        def one_chunk(at, carry):
            place = (1 - half) * rows + at * chunk
            here = pl.ds(pl.multiple_of(place, chunk), chunk)
            code = code_ref[here, :]
            allowed = (code >= low) & (code <= high)
            for group in range(kv_heads):
                cols = slice(group * HEAD_DIM, (group + 1) * HEAD_DIM)
                value_cols = slice((kv_heads + group) * HEAD_DIM, (kv_heads + group + 1) * HEAD_DIM)
                keys = kv_ref[aligned(at, chunk), cols]
                values = kv_ref[aligned(at, chunk), value_cols]
                grad_key = jnp.zeros((chunk, HEAD_DIM), f32)
                grad_value = jnp.zeros((chunk, HEAD_DIM), f32)
                for head in range(group * rep_count, (group + 1) * rep_count):
                    head_cols = slice(head * HEAD_DIM, (head + 1) * HEAD_DIM)
                    query = q_ref[:, head_cols]
                    do = do_ref[:, head_cols]
                    scores = matmul_nt(keys, query)
                    prob = jnp.where(
                        allowed,
                        jnp.exp2(scores * (LOG2E * scale) - lse_ref[head : head + 1, :]),
                        0.0,
                    )
                    grad_prob = matmul_nt(values, do)
                    grad_score = (prob * (grad_prob - delta_ref[head : head + 1, :])).astype(bf16)
                    grad_value += matmul(prob.astype(bf16), do)
                    grad_key += matmul(grad_score, query)
                    dqt_ref[head] += matmul(kt_ref[group, :, here], grad_score)
                dkv_ref[aligned(at, chunk), cols] = (grad_key * scale).astype(dkv_ref.dtype)
                dkv_ref[aligned(at, chunk), value_cols] = grad_value.astype(dkv_ref.dtype)
            return carry

        lax.fori_loop(0, rows // chunk, one_chunk, 0)
    for head in range(heads):
        dq_out[:, head * HEAD_DIM : (head + 1) * HEAD_DIM] = jnp.transpose(dqt_ref[head]) * scale


def project_back(
    ids, dq_ref, dkv_ref, got_ref, dlogit_ref, raw_ref, rows_ref, cos_ref, sin_ref, normed_ref,
    w_ref, ln2_ref, kept, sent, grad_out, turned_ref,
):
    q_cols, kv_cols = dq_ref.shape[1], dkv_ref.shape[1] // 2
    model = normed_ref.shape[1]
    cos, sin = cos_ref[...], sin_ref[...]
    gain_terms = [jnp.zeros((1, HEAD_DIM), f32), jnp.zeros((1, HEAD_DIM), f32)]
    for head in range((q_cols + kv_cols) // HEAD_DIM):
        cols = slice(head * HEAD_DIM, (head + 1) * HEAD_DIM)
        if head * HEAD_DIM < q_cols:
            which, grad = 0, dq_ref[:, cols]
        else:
            kv_at = slice(head * HEAD_DIM - q_cols, (head + 1) * HEAD_DIM - q_cols)
            which, grad = 1, dkv_ref[:, kv_at] + got_ref[:, kv_at].astype(f32)
        grad = grad * cos + pltpu.roll(grad * sin, HEAD_DIM // 2, 1)
        raw = raw_ref[:, cols]
        scale = lax.rsqrt(jnp.mean(raw * raw, axis=-1, keepdims=True) + EPS)
        unit = raw * scale
        gain_terms[which] += jnp.sum(grad * unit, axis=0, keepdims=True)
        gained = grad * rows_ref[2 + which : 3 + which, :HEAD_DIM]
        grad_out[:, cols] = (
            scale * (gained - unit * jnp.mean(gained * unit, axis=-1, keepdims=True))
        ).astype(bf16)
    grad_out[:, q_cols + kv_cols : q_cols + 2 * kv_cols] = (
        dkv_ref[:, kv_cols:] + got_ref[:, kv_cols:].astype(f32)
    ).astype(bf16)
    grad_out[:, q_cols + 2 * kv_cols :] = dlogit_ref[...]
    turned_ref[...] = jnp.transpose(normed_ref[...])
    half = kept.shape[1]
    places = short_places(2 * half * 4)
    wide = q_cols + 2 * kv_cols
    lane = iota((2 * half, LANE), 1)
    for chip in range(4):
        at = slice(chip * 2 * half, (chip + 1) * 2 * half)
        term = matmul(turned_ref[at, :], grad_out[...])
        weights = w_ref[at, :].astype(f32)
        ln1_column = jnp.sum(weights[:, :wide] * term[:, :wide], axis=1, keepdims=True) + jnp.sum(
            jnp.where(lane < HEADS, weights[:, wide:] * term[:, wide:], 0.0), axis=1, keepdims=True
        )
        ln1_column = ln1_column / weights[:, wide + LN1_AT : wide + LN1_AT + 1]
        ln2_column = column_of(ln2_ref[0:1, at])
        small = term[:, wide:]
        small = jnp.where(lane == LN1_AT, ln1_column, small)
        small = jnp.where(lane == LN2_AT, ln2_column, small)
        for which, small_at in ((0, QN_AT), (1, KN_AT)):
            column = jnp.sum(
                jnp.where(places[at, :], gain_terms[which], 0.0), axis=1, keepdims=True
            )
            small = jnp.where(lane == small_at, column, small)
        keep_or_send(
            ids, term[:half, :wide], term[half:, :wide], kept.at[chip, :, :wide], sent.at[chip, :, :wide]
        )
        keep_or_send(
            ids, small[:half], small[half:], kept.at[chip, :, wide:], sent.at[chip, :, wide:]
        )


def project_cot(ids, grad_ref, w_ref, *parts):
    block = parts[0].shape[0]
    for k, part in enumerate(parts):
        part[...] = matmul_nt(grad_ref[k * block : (k + 1) * block, :], w_ref[...]).astype(bf16)


def spread_attention(ids, *refs):
    pieces, (q_out, k_out, v_out, logit_out, ln1_out, ln2_out, qn_out, kn_out) = refs[:4], refs[4:]
    q_cols, kv_cols = q_out.shape[1] // 4, k_out.shape[1] // 4
    for k in range(4):
        chip = ids[0] ^ k
        q_out[:, aligned(chip, q_cols)] = pieces[k][:, :q_cols].astype(f32)
        k_out[:, aligned(chip, kv_cols)] = pieces[k][:, q_cols : q_cols + kv_cols].astype(f32)
        v_out[:, aligned(chip, kv_cols)] = pieces[k][
            :, q_cols + kv_cols : q_cols + 2 * kv_cols
        ].astype(f32)
    small = sum(
        [piece[:, q_cols + 2 * kv_cols :].astype(f32) for piece in pieces[1:]],
        pieces[0][:, q_cols + 2 * kv_cols :].astype(f32),
    )
    logit_out[...] = small[:, :HEADS]
    for at, out in ((LN1_AT, ln1_out), (LN2_AT, ln2_out), (QN_AT, qn_out), (KN_AT, kn_out)):
        out[...] = row_of(small[:, at : at + 1])[:, : out.shape[1]]


def tensor_parallel_layer(
    tokens,
    lengths,
    ln1_gain,
    q_weight,
    k_weight,
    v_weight,
    attn_gate_weight,
    q_norm_gain,
    k_norm_gain,
    o_weight,
    ln2_gain,
    gate_weight,
    up_weight,
    down_weight,
    cotangent,
):
    seq_at, plane = lax.axis_index("seq"), lax.axis_index("dp")
    chip, core = seq_at // 2, seq_at % 2
    ids = jnp.stack([chip, core, plane]).astype(jnp.int32)
    block, model = tokens.shape[1:]
    rows = 4 * block
    rows_w = q_weight.shape[0]
    q_cols, kv_cols = q_weight.shape[1] // 4, k_weight.shape[1] // 4
    heads, kv_heads = q_cols // HEAD_DIM, kv_cols // HEAD_DIM
    wide = q_cols + 2 * kv_cols + LANE
    ff_cols = gate_weight.shape[1] // 4
    o_rows, down_rows = o_weight.shape[0], down_weight.shape[0]
    ones = (1, 2, 3)

    def to_chip(value, k):
        return lax.ppermute(value, "seq", [(s, s ^ (2 * k)) for s in range(8)])

    def to_core(value):
        return lax.ppermute(value, "seq", [(s, s ^ 1) for s in range(8)])

    def to_plane(value, e):
        return lax.ppermute(value, "dp", [(d, d ^ e) for d in range(4)])

    def after(value, *others):
        return lax.optimization_barrier((value,) + others)[0]

    def chip_gather(value):
        return [value] + [to_chip(value, k) for k in ones]

    def chip_swap(parts):
        return [parts[0]] + [to_chip(parts[k], k) for k in ones]

    def plane_gather(value, hold=lambda far: far):
        far = to_plane(value, 2)
        return [value, to_plane(value, 1), far, to_plane(hold(far), 1)]

    def plane_reduce(name, parts):
        relayed = on_core(
            pair_sum,
            name,
            ids,
            [value for part in parts for value in (part[2], to_plane(part[3], 1))],
            [(part[2].shape, bf16) for part in parts],
        )
        return relayed, [
            [part[0], to_plane(after(part[1], far), 1), to_plane(far, 2)]
            for part, far in zip(parts, relayed)
        ]

    def with_core(pieces):
        return pieces + [to_core(piece) for piece in pieces]

    token_own, cot_own = tokens[0], cotangent[0]

    packed = on_core(
        pack_attention,
        "pack_attention",
        ids,
        [
            q_weight,
            k_weight,
            v_weight,
            attn_gate_weight,
            ln1_gain.reshape(1, -1),
            ln2_gain.reshape(1, -1),
            q_norm_gain.reshape(1, -1),
            k_norm_gain.reshape(1, -1),
        ],
        [((rows_w, wide), bf16)] * 4,
        [
            ((rows_w, HEADS), bf16),
            ((1, rows_w), bf16),
            ((1, rows_w), bf16),
            ((1, q_norm_gain.shape[0]), bf16),
            ((1, q_norm_gain.shape[0]), bf16),
        ],
        copies=17,
    )
    swapped = chip_swap(packed)
    (qkv_joined,) = on_core(join_four, "join_qkv", ids, swapped, [((4, rows_w, wide), bf16)])
    qkv_planes = plane_gather(qkv_joined)
    qkv_pieces = with_core(qkv_planes)
    token_pieces = chip_gather(after(token_own, *swapped))

    cos_tab, sin_tab, key_code, limits = on_core(
        positions,
        "positions",
        ids,
        [lengths],
        [
            ((rows, HEAD_DIM), f32),
            ((rows, HEAD_DIM), f32),
            ((2 * rows, 1), jnp.int32),
            ((8, rows), jnp.int32),
        ],
        scalars=2,
    )

    weights, normed, raw, queries, own_kv, gates, gain_rows = on_core(
        project,
        "project",
        ids,
        token_pieces + qkv_pieces + [cos_tab, sin_tab],
        [
            ((model, wide), bf16),
            ((rows, model), bf16),
            ((rows, q_cols + kv_cols), f32),
            ((rows, q_cols), bf16),
            ((rows, 2 * kv_cols), bf16),
            ((rows, LANE), f32),
            ((8, model), f32),
        ],
    )
    other_kv = to_core(own_kv)

    o_planes = plane_gather(after(o_weight, qkv_planes[2]))
    o_pieces = with_core(o_planes)

    ff_packed = on_core(
        pack_forward,
        "pack_forward",
        ids,
        [gate_weight, up_weight],
        [((rows_w, 2 * ff_cols), bf16)] * 4,
        copies=8,
    )
    ff_swapped = chip_swap([after(piece, qkv_planes[3]) for piece in ff_packed])
    cot_pieces = chip_gather(after(cot_own, qkv_planes[2]))
    (ff_stack,) = on_core(join_four, "join_ff", ids, ff_swapped, [((4, rows_w, 2 * ff_cols), bf16)])

    *o_parts, attended, gated, lse, o_whole = on_core(
        attend,
        "attend",
        ids,
        [queries, own_kv, other_kv, gates, key_code, limits] + o_pieces,
        [((block, model), bf16)] * 4
        + [
            ((rows, q_cols), f32),
            ((rows, q_cols), bf16),
            ((8, rows), f32),
            ((8 * o_rows, model), bf16),
        ],
        [
            ((kv_heads, HEAD_DIM, 2 * rows), bf16),
            ((heads, HEAD_DIM, rows), f32),
            ((8, rows), f32),
        ],
    )
    o_got = chip_swap(o_parts)
    ff_planes = plane_gather(ff_stack, lambda far: after(far, o_got[1]))
    hidden, normed_two = on_core(
        join_hidden,
        "join_hidden",
        ids,
        [token_own, gain_rows] + o_got,
        [((block, model), f32), ((block, model), bf16)],
    )
    down_planes = plane_gather(after(down_weight, attended), lambda far: after(far, normed_two))
    ff_pieces, down_pieces = with_core(ff_planes), with_core(down_planes)
    *two_parts, acted, ff_cot, normed_two_all, cot_all, down_whole = on_core(
        feed_forward,
        "feed_forward",
        ids,
        chip_gather(normed_two) + cot_pieces + ff_pieces + down_pieces,
        [((block, model), bf16)] * 4
        + [
            ((rows, ff_cols), bf16),
            ((rows, 2 * ff_cols), bf16),
            ((rows, model), bf16),
            ((rows, model), bf16),
            ((8 * down_rows, model), bf16),
        ],
        [((model, 2 * ff_cols), bf16)],
    )
    two_got = chip_swap(two_parts)
    ff_kept, ff_sent, down_kept, down_sent = on_core(
        forward_grads,
        "forward_grads",
        ids,
        [acted, ff_cot, normed_two_all, cot_all],
        [
            ((4, 4 * rows_w, 2 * ff_cols), bf16),
            ((4, 4 * rows_w, 2 * ff_cols), bf16),
            ((4 * down_rows, model), bf16),
            ((4 * down_rows, model), bf16),
        ],
        [((model, rows), bf16), ((ff_cols, rows), bf16)],
    )
    out_parts = on_core(
        forward_out, "forward_out", ids, [acted, down_whole], [((block, model), bf16)] * 4
    )
    two_got = [two_got[0]] + [after(value, ff_sent) for value in two_got[1:]]
    hidden_grad, hidden_grad_b, ln2_row = on_core(
        second_norm_back,
        "second_norm_back",
        ids,
        [hidden, cot_own, gain_rows] + two_got,
        [((block, model), f32), ((block, model), bf16), ((8, model), f32)],
    )
    ff_halves = on_core(
        core_sum_forward,
        "core_sum_forward",
        ids,
        [ff_kept, to_core(ff_sent), down_kept, to_core(down_sent)],
        [((4, rows_w, 2 * ff_cols), bf16)] * 4 + [((down_rows, model), bf16)] * 4,
    )
    ff_relayed, (ff_totals, down_totals) = plane_reduce(
        "relay_forward", [ff_halves[:4], ff_halves[4:]]
    )
    grad_pieces = chip_gather(hidden_grad_b)
    out_got = chip_swap([after(part, *grad_pieces) for part in out_parts])
    grad_pieces = grad_pieces[:1] + [after(value, *ff_relayed, *out_parts) for value in grad_pieces[1:]]

    dq, dkv_own, dkv_other, dlogit, hidden_grad_all = on_core(
        attend_back,
        "attend_back",
        ids,
        grad_pieces
        + [o_whole, attended, gates, queries, own_kv, other_kv, lse, key_code, limits],
        [
            ((rows, q_cols), f32),
            ((rows, 2 * kv_cols), f32),
            ((rows, 2 * kv_cols), bf16),
            ((rows, LANE), bf16),
            ((rows, model), bf16),
        ],
        [
            ((rows, q_cols), bf16),
            ((8, rows), f32),
            ((kv_heads, HEAD_DIM, 2 * rows), bf16),
            ((heads, HEAD_DIM, rows), f32),
        ],
    )
    dkv_got = to_core(dkv_other)
    o_kept, o_sent = on_core(
        o_grads,
        "o_grads",
        ids,
        [gated, hidden_grad_all],
        [((4 * o_rows, model), bf16)] * 2,
        [((q_cols, rows), bf16)],
    )
    (layer_out,) = on_core(join_out, "join_out", ids, [hidden] + out_got, [((block, model), bf16)])
    o_halves = on_core(
        core_sum_one, "core_sum_o", ids, [o_kept, to_core(o_sent)], [((o_rows, model), bf16)] * 4
    )
    dkv_got = after(dkv_got, o_sent)

    qkv_kept, qkv_sent, qkv_cot = on_core(
        project_back,
        "project_back",
        ids,
        [dq, dkv_own, dkv_got, dlogit, raw, gain_rows, cos_tab, sin_tab, normed, weights, ln2_row],
        [((4, 4 * rows_w, wide), bf16), ((4, 4 * rows_w, wide), bf16), ((rows, wide), bf16)],
        [((model, rows), bf16)],
    )
    one_parts = on_core(
        project_cot, "project_cot", ids, [qkv_cot, weights], [((block, model), bf16)] * 4
    )
    qkv_halves = on_core(
        core_sum_one,
        "core_sum_qkv",
        ids,
        [qkv_kept, after(to_core(qkv_sent), *ff_totals[1:], *down_totals[1:])],
        [((4, rows_w, wide), bf16)] * 4,
    )
    unused_relay, (qkv_totals, o_totals) = plane_reduce("relay_attention", [qkv_halves, o_halves])

    ff_columns = on_core(
        plane_sum_columns, "plane_sum_ff", ids, ff_totals, [((rows_w, 2 * ff_cols), bf16)] * 4
    )
    gate_grad, up_grad = on_core(
        spread_forward,
        "spread_forward",
        ids,
        chip_swap(ff_columns),
        [((rows_w, 4 * ff_cols), f32)] * 2,
    )
    (down_grad,) = on_core(
        plane_sum_rows, "plane_sum_down", ids, down_totals, [((down_rows, model), f32)]
    )
    (o_grad,) = on_core(plane_sum_rows, "plane_sum_o", ids, o_totals, [((o_rows, model), f32)])
    (grad_input,) = on_core(
        first_norm_back,
        "first_norm_back",
        ids,
        [token_own, hidden_grad, gain_rows] + chip_swap(one_parts),
        [((block, model), f32)],
    )
    qkv_columns = on_core(
        plane_sum_columns, "plane_sum_qkv", ids, qkv_totals, [((rows_w, wide), bf16)] * 4
    )
    gain_len = q_norm_gain.shape[0]
    q_grad, k_grad, v_grad, logit_grad, ln1_grad, ln2_grad, qn_grad, kn_grad = on_core(
        spread_attention,
        "spread_attention",
        ids,
        chip_swap(qkv_columns),
        [
            ((rows_w, 4 * q_cols), f32),
            ((rows_w, 4 * kv_cols), f32),
            ((rows_w, 4 * kv_cols), f32),
            ((rows_w, HEADS), f32),
            ((1, rows_w), f32),
            ((1, rows_w), f32),
            ((1, gain_len), f32),
            ((1, gain_len), f32),
        ],
    )
    return (
        layer_out[None],
        grad_input[None],
        ln1_grad.reshape(-1),
        q_grad,
        k_grad,
        v_grad,
        logit_grad,
        qn_grad.reshape(-1),
        kn_grad.reshape(-1),
        o_grad,
        ln2_grad.reshape(-1),
        gate_grad,
        up_grad,
        down_grad,
    )


def solution(mesh):
    split_heads = mesh.shape["seq"] == 8 and mesh.shape["dp"] == 4
    in_specs = (
        P("dp", "seq", None),
        P("dp", None),
        P(("seq", "dp")),
        P(("seq", "dp"), None),
        P(("seq", "dp"), None),
        P(("seq", "dp"), None),
        P(("seq", "dp"), None),
        P(("seq", "dp")),
        P(("seq", "dp")),
        P(("seq", "dp"), None),
        P(("seq", "dp")),
        P(("seq", "dp"), None),
        P(("seq", "dp"), None),
        P(("seq", "dp"), None),
        P("dp", "seq", None),
    )
    out_specs = (
        P("dp", "seq", None),
        P("dp", "seq", None),
        P(("seq", "dp")),
        P(("seq", "dp"), None),
        P(("seq", "dp"), None),
        P(("seq", "dp"), None),
        P(("seq", "dp"), None),
        P(("seq", "dp")),
        P(("seq", "dp")),
        P(("seq", "dp"), None),
        P(("seq", "dp")),
        P(("seq", "dp"), None),
        P(("seq", "dp"), None),
        P(("seq", "dp"), None),
    )
    return jax.shard_map(
        tensor_parallel_layer if split_heads else gathered_layer,
        mesh=mesh, in_specs=in_specs, out_specs=out_specs, check_vma=False
    )
```
